32 devices in a mesh: groups: 2 (over y), vocab: 4 (over z), rows: 2 (over x), teach: 2 (over core).
Axes of the slice: x: 2, y: 2, z: 4, core: 2. Of those that a mesh axis runs over, the one named last changes fastest.
Arguments:
- hidden_rows: bfloat16 [32, 3584], P(('groups', 'vocab')), parts along dimension 0, may hold values from -512 to 512
- mentor_unnormalized: float32 [32, 4864], P(('groups', 'teach'), ('vocab', 'rows')), parts along dimension 0, may hold values from -1000 to 1000
- head_weight: bfloat16 [4864, 3584], P(('vocab', 'rows', 'teach')), may hold values from -2 to 2
- row_mask: int32 [32], P('groups'), parts along dimension 0, may hold values 0 or 1
Outputs:
- divergence: float32 [32], P('groups'), parts along dimension 0
- hidden_grad: bfloat16 [32, 3584], P(('groups', 'vocab', 'rows', 'teach')), parts along dimension 0
- weight_grad: bfloat16 [9728, 3584], P(('groups', 'vocab', 'rows', 'teach')), parts along dimension 0
The draws below stay inside these ranges and needn't reach their ends.
There are 2 independent parts, one for each index of `groups`. The reference program is written for one: setup_inputs(seed, part) draws one part's arguments, and reference() takes and returns one part's arrays. A program takes and returns all parts, laid end to end along the dimension named above; an argument that names none is the same for every part. Nothing has to cross between parts.
All inputs are finite; a program needn't handle non-finite values.
Results may differ from the reference program's by a relative error of at most 0.0051.
Values may be sent and summed in bfloat16 or wider, within the bound.
No kernel may reach another device: no remote copies, remote signals or barrier semaphores. Data moves between devices by JAX's collectives and lax.ppermute only.
A program may use at most 64 MiB of HBM per device.

```python
import math
import jax
import jax.numpy as jnp

D = 3584
V = 4864
ROWS = 16


def draw_hidden_rows(key, part):
    first, second = jax.random.split(key, 2)
    scales = jnp.exp(jax.random.uniform(second, (ROWS, 1), jnp.float32, math.log(0.3), math.log(3.0)))
    result = jnp.clip(jax.random.normal(first, (ROWS, D), jnp.float32), -4.0, 4.0) * scales
    return result.astype(jnp.bfloat16)


def draw_mentor_unnormalized(key, part):
    first = jax.random.fold_in(key, 0)
    position = jnp.arange(V).astype(jnp.float32)[None, :] / V
    ramp = 2.0 * jnp.log(1.0 + 2.0 * position)
    values = jnp.clip(jax.random.normal(first, (ROWS, V), jnp.float32), -4.0, 4.0)
    result = 4.0 * values + ramp
    return result.astype(jnp.float32)


def draw_head_weight(key, part):
    first = jax.random.fold_in(key, 0)
    weight_scale = 3.0 / math.sqrt(D)
    values = jnp.clip(jax.random.normal(first, (V, D), jnp.float32), -4.0, 4.0)
    return (values * weight_scale).astype(jnp.bfloat16)


def plant(entries, rng, smallest, largest):
    spot = [jax.random.randint(jax.random.fold_in(rng, axis), (), 0, length) for axis, length in enumerate(entries.shape)]
    main_axis = entries.shape.index(max(entries.shape))
    beside = spot[:main_axis] + [(spot[main_axis] + 1) % entries.shape[main_axis]] + spot[main_axis + 1:]
    return entries.at[tuple(spot)].set(smallest).at[tuple(beside)].set(largest)


def setup_inputs(seed: int = 0, part: int = 0) -> dict:
    streams_of = jax.random.split(jax.random.key(seed), 5)
    own_keys = jax.random.split(jax.random.fold_in(streams_of[4], part), 5)
    hidden_rows = draw_hidden_rows(jax.random.fold_in(jax.random.fold_in(streams_of[4], part), 71), part)
    mentor_unnormalized = draw_mentor_unnormalized(jax.random.fold_in(jax.random.fold_in(streams_of[4], part), 71), part)
    head_weight = draw_head_weight(jax.random.fold_in(streams_of[4], 71), part)
    row_mask = plant((jax.random.randint(own_keys[3], (ROWS,), 0, 4) < 3).astype(jnp.int32), jax.random.fold_in(own_keys[3], 1), 0, 1)
    return {"hidden_rows": hidden_rows, "mentor_unnormalized": mentor_unnormalized, "head_weight": head_weight, "row_mask": row_mask}


smoothing_divisor = 2.0
objective_scale = 256.0


def reference(hidden_rows, mentor_unnormalized, head_weight, row_mask):
    head_product_matrix = jnp.dot(hidden_rows, head_weight.T, preferred_element_type=jnp.float32)
    learner_unnormalized = head_product_matrix / smoothing_divisor
    divided_learner_values = mentor_unnormalized / smoothing_divisor
    max_student = jnp.max(learner_unnormalized, axis=1)
    sum_student = jnp.sum(jnp.exp(learner_unnormalized - max_student[:, None]), axis=1)
    lse_student = max_student + jnp.log(sum_student)
    max_teacher = jnp.max(divided_learner_values, axis=1)
    sum_teacher = jnp.sum(jnp.exp(divided_learner_values - max_teacher[:, None]), axis=1)
    lse_teacher = max_teacher + jnp.log(sum_teacher)
    mentor_softmax = jnp.exp(divided_learner_values - lse_teacher[:, None])
    learner_softmax = jnp.exp(learner_unnormalized - lse_student[:, None])
    valid_token_count = row_mask.astype(jnp.float32)
    divergence = valid_token_count * (jnp.sum(mentor_softmax * (divided_learner_values - learner_unnormalized), axis=1) - lse_teacher + lse_student)
    raw_score_derivative = (valid_token_count[:, None] * (objective_scale * smoothing_divisor) * (learner_softmax - mentor_softmax)).astype(jnp.bfloat16)
    hidden_grad = jnp.dot(raw_score_derivative, head_weight, preferred_element_type=jnp.float32).astype(jnp.bfloat16)
    weight_grad = jnp.dot(raw_score_derivative.T, hidden_rows, preferred_element_type=jnp.float32).astype(jnp.bfloat16)
    return (divergence, hidden_grad, weight_grad)
```

```python
import jax
import jax.numpy as jnp
from jax import lax
from jax.sharding import PartitionSpec as P

smoothing_divisor = 2.0
objective_scale = 256.0


def flip(n, d):
    return [(i, i ^ d) for i in range(n)]


def bits(n):
    out = []
    d = 1
    while d < n:
        out.append(d)
        d *= 2
    return out


def swap(a, d):
    n = a.shape[0]
    b = a.reshape((n // (2 * d), 2, d) + a.shape[1:])
    return jnp.concatenate([b[:, 1:], b[:, :1]], axis=1).reshape(a.shape)


def relative(a, position, n, stride):
    for d in bits(n):
        a = jnp.where((position & d) != 0, swap(a, d * stride), a)
    return a


def make_body(nz, nx, nc):
    def body(hidden_rows, mentor, head_weight, row_mask):
        z, x, c = lax.axis_index("vocab"), lax.axis_index("rows"), lax.axis_index("teach")
        total = row_mask.shape[0]
        q = total // (nz * nx * nc)
        own = relative(relative(hidden_rows, c, nc, q), x, nx, q * nc)
        gathered = own
        if nz == 4:
            gathered = jnp.concatenate(
                [own] + [lax.ppermute(own, "vocab", flip(nz, k)) for k in (1, 2, 3)], 0
            )
        else:
            for d in bits(nz):
                gathered = jnp.concatenate([gathered, lax.ppermute(gathered, "vocab", flip(nz, d))], 0)
        width = mentor.shape[1] // 2
        left, right = mentor[:, :width], mentor[:, width:]
        kept = jnp.where(c == 0, left, right)
        got = lax.ppermute(jnp.where(c == 0, right, left), "teach", flip(nc, 1))
        scaled = jnp.concatenate([jnp.where(c == 0, kept, got), jnp.where(c == 0, got, kept)], 0)

        def rel(a):
            a = relative(a, c, nc, q)
            a = relative(a, x, nx, q * nc)
            return relative(a, z, nz, q * nc * nx)

        scaled = rel(scaled) / smoothing_divisor
        mask = rel(row_mask).astype(jnp.float32)
        student = (
            lax.dot_general(
                gathered, head_weight, (((1,), (1,)), ((), ())), preferred_element_type=jnp.float32
            )
            / smoothing_divisor
        )
        ms = jnp.max(student, axis=1)
        mt = jnp.max(scaled, axis=1)
        es = jnp.exp(student - ms[:, None])
        et = jnp.exp(scaled - mt[:, None])
        stats = jnp.stack(
            [ms, mt, jnp.sum(es, axis=1), jnp.sum(et, axis=1), jnp.sum(et * (scaled - student), axis=1)], 0
        )
        both = jnp.concatenate([es, et], 0)
        high = both.astype(jnp.bfloat16)
        low = (both - high.astype(jnp.float32)).astype(jnp.bfloat16)
        part = jnp.dot(
            jnp.concatenate([high, low], 0), head_weight, preferred_element_type=jnp.float32
        )
        part = part[: 2 * total] + part[2 * total :]
        part = part.reshape(2, nz, nx, nc, q, -1)

        def merge(keep, stats, others):
            top = stats[:2]
            for _, s in others:
                top = jnp.maximum(top, s[:2])
            factor = [jnp.exp(s[:2] - top) for s in [stats] + [s for _, s in others]]
            sums = sum(
                jnp.concatenate([f * s[2:4], (f[1] * s[4])[None]], 0)
                for f, s in zip(factor, [stats] + [s for _, s in others])
            )
            return top, factor, jnp.concatenate([top, sums], 0)

        def level(part, stats, axis, n, dim, stride):
            if n == 4:
                steps = [(1, 2, 3)]
            else:
                steps = [(d,) for d in reversed(bits(n))]
            size = n
            for ds in steps:
                span = size // (len(ds) + 1)
                keep = lax.slice_in_dim(part, 0, span, axis=dim)
                others = []
                for d in ds:
                    a = lax.ppermute(lax.slice_in_dim(part, d, d + span, axis=dim), axis, flip(n, d))
                    s = lax.ppermute(stats, axis, flip(n, d))
                    s = s.T
                    for b in bits(n):
                        if d & b:
                            s = swap(s, b * stride)
                    others.append((a, s.T))
                _, factor, stats = merge(keep, stats, others)
                rows = [f.reshape(2, nz, nx, nc, q, 1) for f in factor]

                def cut(f):
                    shape = keep.shape
                    for ax in range(1, 4):
                        f = lax.slice_in_dim(f, 0, shape[ax], axis=ax)
                    return f

                part = keep * cut(rows[0])
                for (a, _), f in zip(others, rows[1:]):
                    part = part + a * cut(f)
                size = span
            return part, stats

        part, stats = level(part, stats, "teach", nc, 3, q)
        part, stats = level(part, stats, "rows", nx, 2, q * nc)
        part, stats = level(part, stats, "vocab", nz, 1, q * nc * nx)
        part = part.reshape(2, q, -1)
        ms, mt, ls, lt, cross = stats
        lse_s = ms + jnp.log(ls)
        lse_t = mt + jnp.log(lt)
        divergence = rel(mask * (cross / lt - lse_t + lse_s))
        gain = mask * (objective_scale * smoothing_divisor)
        grad = (
            gain[:, None] * (jnp.exp(student - lse_s[:, None]) - jnp.exp(scaled - lse_t[:, None]))
        ).astype(jnp.bfloat16)
        weight_grad = lax.dot_general(
            grad, gathered, (((0,), (0,)), ((), ())), preferred_element_type=jnp.float32
        )
        hidden_grad = gain[:q, None] * (part[0] / ls[:q, None] - part[1] / lt[:q, None])
        return divergence, hidden_grad.astype(jnp.bfloat16), weight_grad.astype(jnp.bfloat16)

    return body


def solution(mesh):
    body = make_body(mesh.shape["vocab"], mesh.shape["rows"], mesh.shape["teach"])
    return jax.shard_map(
        body,
        mesh=mesh,
        in_specs=(
            P(("groups", "vocab"), None),
            P(("groups", "teach"), ("vocab", "rows")),
            P(("vocab", "rows", "teach"), None),
            P("groups"),
        ),
        out_specs=(
            P("groups"),
            P(("groups", "vocab", "rows", "teach"), None),
            P(("groups", "vocab", "rows", "teach"), None),
        ),
        check_vma=False,
    )
```

```python
import jax
import jax.numpy as jnp
from jax import lax
from jax.experimental import pallas as pl
from jax.experimental.pallas import tpu as pltpu
from jax.sharding import PartitionSpec as P

smoothing_divisor = 2.0
objective_scale = 256.0


def flip(n, d):
    return [(i, i ^ d) for i in range(n)]


def bits(n):
    out = []
    d = 1
    while d < n:
        out.append(d)
        d *= 2
    return out


def swap(a, d):
    n = a.shape[0]
    b = a.reshape((n // (2 * d), 2, d) + a.shape[1:])
    return jnp.concatenate([b[:, 1:], b[:, :1]], axis=1).reshape(a.shape)


def relative(a, position, n, stride):
    for d in bits(n):
        a = jnp.where((position & d) != 0, swap(a, d * stride), a)
    return a


def make_body(nz, nx, nc):
    def body(hidden_rows, mentor, head_weight, row_mask):
        z, x, c = lax.axis_index("vocab"), lax.axis_index("rows"), lax.axis_index("teach")
        total = row_mask.shape[0]
        q = total // (nz * nx * nc)
        own = relative(relative(hidden_rows, c, nc, q), x, nx, q * nc)
        gathered = own
        if nz == 4:
            gathered = jnp.concatenate(
                [own] + [lax.ppermute(own, "vocab", flip(nz, k)) for k in (1, 2, 3)], 0
            )
        else:
            for d in bits(nz):
                gathered = jnp.concatenate([gathered, lax.ppermute(gathered, "vocab", flip(nz, d))], 0)
        width = mentor.shape[1] // 2
        left, right = mentor[:, :width], mentor[:, width:]
        kept = jnp.where(c == 0, left, right)
        got = lax.ppermute(jnp.where(c == 0, right, left), "teach", flip(nc, 1))
        scaled = jnp.concatenate([jnp.where(c == 0, kept, got), jnp.where(c == 0, got, kept)], 0)

        def rel(a):
            a = relative(a, c, nc, q)
            a = relative(a, x, nx, q * nc)
            return relative(a, z, nz, q * nc * nx)

        scaled = rel(scaled) / smoothing_divisor
        mask = rel(row_mask).astype(jnp.float32)
        student = (
            lax.dot_general(
                gathered, head_weight, (((1,), (1,)), ((), ())), preferred_element_type=jnp.float32
            )
            / smoothing_divisor
        )
        ms = jnp.max(student, axis=1)
        mt = jnp.max(scaled, axis=1)
        es = jnp.exp(student - ms[:, None])
        et = jnp.exp(scaled - mt[:, None])
        stats = jnp.stack(
            [ms, mt, jnp.sum(es, axis=1), jnp.sum(et, axis=1), jnp.sum(et * (scaled - student), axis=1)], 0
        )
        both = jnp.concatenate([es, et], 0)
        high = both.astype(jnp.bfloat16)
        low = (both - high.astype(jnp.float32)).astype(jnp.bfloat16)
        part = jnp.dot(
            jnp.concatenate([high, low], 0), head_weight, preferred_element_type=jnp.float32
        )
        part = part[: 2 * total] + part[2 * total :]
        part = part.reshape(2, nz, nx, nc, q, -1)

        def merge(keep, stats, others):
            top = stats[:2]
            for _, s in others:
                top = jnp.maximum(top, s[:2])
            factor = [jnp.exp(s[:2] - top) for s in [stats] + [s for _, s in others]]
            sums = sum(
                jnp.concatenate([f * s[2:4], (f[1] * s[4])[None]], 0)
                for f, s in zip(factor, [stats] + [s for _, s in others])
            )
            return top, factor, jnp.concatenate([top, sums], 0)

        def level(part, stats, axis, n, dim, stride):
            if n == 4:
                steps = [(1, 2, 3)]
            else:
                steps = [(d,) for d in reversed(bits(n))]
            size = n
            for ds in steps:
                span = size // (len(ds) + 1)
                keep = lax.slice_in_dim(part, 0, span, axis=dim)
                others = []
                for d in ds:
                    a = lax.ppermute(lax.slice_in_dim(part, d, d + span, axis=dim), axis, flip(n, d))
                    s = lax.ppermute(stats, axis, flip(n, d))
                    s = s.T
                    for b in bits(n):
                        if d & b:
                            s = swap(s, b * stride)
                    others.append((a, s.T))
                _, factor, stats = merge(keep, stats, others)
                rows = [f.reshape(2, nz, nx, nc, q, 1) for f in factor]

                def cut(f):
                    shape = keep.shape
                    for ax in range(1, 4):
                        f = lax.slice_in_dim(f, 0, shape[ax], axis=ax)
                    return f

                part = keep * cut(rows[0])
                for (a, _), f in zip(others, rows[1:]):
                    part = part + a * cut(f)
                size = span
            return part, stats

        part, stats = level(part, stats, "teach", nc, 3, q)
        part, stats = level(part, stats, "rows", nx, 2, q * nc)
        part, stats = level(part, stats, "vocab", nz, 1, q * nc * nx)
        part = part.reshape(2, q, -1)
        ms, mt, ls, lt, cross = stats
        lse_s = ms + jnp.log(ls)
        lse_t = mt + jnp.log(lt)
        divergence = rel(mask * (cross / lt - lse_t + lse_s))
        gain = mask * (objective_scale * smoothing_divisor)
        grad = (
            gain[:, None] * (jnp.exp(student - lse_s[:, None]) - jnp.exp(scaled - lse_t[:, None]))
        ).astype(jnp.bfloat16)
        weight_grad = lax.dot_general(
            grad, gathered, (((0,), (0,)), ((), ())), preferred_element_type=jnp.float32
        )
        hidden_grad = gain[:q, None] * (part[0] / ls[:q, None] - part[1] / lt[:q, None])
        return divergence, hidden_grad.astype(jnp.bfloat16), weight_grad.astype(jnp.bfloat16)

    return body


ROWS = 16
STATS = 128


def pack(columns):
    lane = lax.broadcasted_iota(jnp.int32, (ROWS, STATS), 1)
    out = jnp.zeros((ROWS, STATS), jnp.float32)
    for i, column in enumerate(columns):
        out = jnp.where(lane == i, column, out)
    return out


def unite(parts):
    top = parts[0]
    for s in parts[1:]:
        top = jnp.maximum(top, s)
    factors = [jnp.exp(s - top) for s in parts]
    ls = sum(s[:, 2:3] * f[:, 0:1] for s, f in zip(parts, factors))
    lt = sum(s[:, 3:4] * f[:, 1:2] for s, f in zip(parts, factors))
    cross = sum(s[:, 4:5] * f[:, 1:2] for s, f in zip(parts, factors))
    return factors, [top[:, 0:1], top[:, 1:2], ls, lt, cross]


def places():
    return lax.axis_index("vocab"), lax.axis_index("rows"), lax.axis_index("teach")


def row_of(b, x, c):
    return 2 * (x ^ (b & 1)) + (c ^ (b >> 1))


def first_kernel(h0, h1, h2, h3, w, own_t, got_t, student, scaled, stats, keep, send, hf, raw, tt, e):
    z, x, c = places()
    for k, h in enumerate((h0, h1, h2, h3)):
        hf[4 * k : 4 * k + 4, :] = h[...].astype(jnp.float32)
    raw[...] = 0.5 * lax.dot_general(
        hf[...].astype(jnp.bfloat16), w[...], (((1,), (1,)), ((), ())), preferred_element_type=jnp.float32
    )
    tt[pl.ds(8 * c, 8), :] = own_t[...]
    tt[pl.ds(8 * (1 - c), 8), :] = got_t[...]
    for b in range(4):
        j = row_of(b, x, c)
        for k in range(4):
            student[4 * b + k : 4 * b + k + 1, :] = raw[pl.ds(4 * k + j, 1), :]
            scaled[4 * b + k : 4 * b + k + 1, :] = 0.5 * tt[pl.ds(4 * (k ^ z) + j, 1), :]
    s = student[...]
    t = scaled[...]
    ms = jnp.max(s, axis=1, keepdims=True)
    mt = jnp.max(t, axis=1, keepdims=True)
    es = jnp.exp(s - ms)
    et = jnp.exp(t - mt)
    st = pack(
        [
            ms,
            mt,
            jnp.sum(es, axis=1, keepdims=True),
            jnp.sum(et, axis=1, keepdims=True),
            jnp.sum(et * (t - s), axis=1, keepdims=True),
        ]
    )
    stats[...] = st
    for b in range(4):
        e[8 * b : 8 * b + 4, :] = es[4 * b : 4 * b + 4, :]
        e[8 * b + 4 : 8 * b + 8, :] = et[4 * b : 4 * b + 4, :]
    both = e[...]
    high = both.astype(jnp.bfloat16)
    low = (both - high.astype(jnp.float32)).astype(jnp.bfloat16)
    part = jnp.dot(jnp.concatenate([high, low], 0), w[...], preferred_element_type=jnp.float32)
    d = part.shape[1]
    keep[...] = part[0:16] + part[32:48]
    send[:, 0:d] = part[16:32] + part[48:64]
    send[0:8, d:] = st[8:16]
    send[8:16, d:] = st[0:8]


def second_kernel(part, stats, got, stats_out, keep, send):
    d = part.shape[1]
    factors, columns = unite([stats[...], got[:, d:]])
    st = pack(columns)
    stats_out[...] = st
    scale = [
        jnp.concatenate([f[0:4, 0:1], f[0:4, 1:2], f[4:8, 0:1], f[4:8, 1:2]], 0) for f in factors
    ]
    total = part[...] * scale[0] + got[:, 0:d] * scale[1]
    keep[...] = total[0:8]
    send[:, 0:d] = total[8:16]
    for i in range(2):
        send[0:4, d + 128 * i : d + 128 * i + 128] = st[8 * i + 4 : 8 * i + 8]
        send[4:8, d + 128 * i : d + 128 * i + 128] = st[8 * i : 8 * i + 4]


def third_kernel(part, stats, got, stats_out, keep, send1, send2, send3, gs):
    d = part.shape[1]
    for i in range(2):
        gs[8 * i : 8 * i + 8, :] = got[:, d + 128 * i : d + 128 * i + 128]
    factors, columns = unite([stats[...], gs[...]])
    st = pack(columns)
    stats_out[...] = st
    scale = [jnp.concatenate([f[0:4, 0:1], f[0:4, 1:2]], 0) for f in factors]
    total = part[...] * scale[0] + got[:, 0:d] * scale[1]
    keep[0:1, :] = total[0:1]
    keep[1:2, :] = total[4:5]
    for k, send in enumerate((send1, send2, send3), 1):
        send[0:1, 0:d] = total[k : k + 1]
        send[1:2, 0:d] = total[4 + k : 5 + k]
        for p in range(ROWS):
            at = d + 128 * (p // 2)
            r = p ^ k
            send[p % 2 : p % 2 + 1, at : at + 128] = st[r : r + 1]


def make_last_kernel(chunk):
    def last_kernel(
        mask, part, stats, got1, got2, got3, student, scaled, h0, h1, h2, h3,
        divergence, hidden_grad, weight_grad, gs, hf, gr, out, sems,
    ):
        z, x, c = places()
        d = part.shape[1]
        parts = [stats[...]]
        for k, got in enumerate((got1, got2, got3)):
            for i in range(8):
                gs[k, 2 * i : 2 * i + 2, :] = got[:, d + 128 * i : d + 128 * i + 128]
            parts.append(gs[k])
        factors, (ms, mt, ls, lt, cross) = unite(parts)
        lse_s = ms + jnp.log(ls)
        lse_t = mt + jnp.log(lt)
        row = lax.broadcasted_iota(jnp.int32, (ROWS, 1), 0)
        valid = jnp.zeros((ROWS, 1), jnp.float32)
        for r in range(ROWS):
            b, k = r // 4, r % 4
            valid = jnp.where(
                row == r, mask[4 * (k ^ z) + row_of(b, x, c)].astype(jnp.float32), valid
            )
        gain = valid * (objective_scale * smoothing_divisor)
        grad = gain * (jnp.exp(student[...] - lse_s) - jnp.exp(scaled[...] - lse_t))
        for b in range(4):
            j = row_of(b, x, c)
            for k in range(4):
                gr[pl.ds(4 * k + j, 1), :] = grad[4 * b + k : 4 * b + k + 1, :]
        for k, h in enumerate((h0, h1, h2, h3)):
            hf[4 * k : 4 * k + 4, :] = h[...].astype(jnp.float32)
        g = gr[...].astype(jnp.bfloat16)
        copies = []
        for i in range(d // chunk):
            at = pl.ds(i * chunk, chunk)
            out[:, at] = lax.dot_general(
                g,
                hf[:, at].astype(jnp.bfloat16),
                (((0,), (0,)), ((), ())),
                preferred_element_type=jnp.float32,
            ).astype(jnp.bfloat16)
            copy = pltpu.make_async_copy(out.at[:, at], weight_grad.at[:, at], sems.at[i])
            copy.start()
            copies.append(copy)
        home = 4 * (z ^ (row & 3)) + 2 * (x ^ ((row >> 2) & 1)) + (c ^ (row >> 3))
        value = valid * (cross / lt - lse_t + lse_s)
        lane = lax.broadcasted_iota(jnp.int32, (ROWS, STATS), 1)
        divergence[...] = jnp.sum(jnp.where(lane == home, value, 0.0), axis=0, keepdims=True)
        a_s = part[0:1, :] * factors[0][0:1, 0:1]
        a_t = part[1:2, :] * factors[0][0:1, 1:2]
        for got, f in zip((got1, got2, got3), factors[1:]):
            a_s = a_s + got[0:1, 0:d] * f[0:1, 0:1]
            a_t = a_t + got[1:2, 0:d] * f[0:1, 1:2]
        hidden_grad[...] = (
            gain[0:1] * (a_s / ls[0:1] - a_t / lt[0:1])
        ).astype(jnp.bfloat16)
        for copy in copies:
            copy.wait()

    return last_kernel


VMEM = pl.BlockSpec(memory_space=pltpu.VMEM)
SMEM = pl.BlockSpec(memory_space=pltpu.SMEM)
PARAMS = pltpu.CompilerParams(vmem_limit_bytes=32 << 20)


def call(kernel, out, scratch=(), in_specs=None, out_specs=None):
    shapes = [jax.ShapeDtypeStruct(s, t) for s, t in out]
    return lambda *a: pl.pallas_call(
        kernel,
        out_shape=shapes,
        in_specs=in_specs or [VMEM] * len(a),
        out_specs=out_specs or [VMEM] * len(out),
        scratch_shapes=list(scratch),
        compiler_params=PARAMS,
    )(*a)


def small_body(hidden_rows, mentor, head_weight, row_mask):
    f32, bf16 = jnp.float32, jnp.bfloat16
    v, d = head_weight.shape
    c = lax.axis_index("teach")
    pieces = [hidden_rows] + [lax.ppermute(hidden_rows, "vocab", flip(4, k)) for k in (1, 2, 3)]
    left, right = mentor[:, :v], mentor[:, v:]
    got_t = lax.ppermute(jnp.where(c == 0, right, left), "teach", flip(2, 1))
    own_t = jnp.where(c == 0, left, right)
    student, scaled, stats, keep, send = call(
        first_kernel,
        [((ROWS, v), f32), ((ROWS, v), f32), ((ROWS, STATS), f32), ((16, d), f32), ((16, d + STATS), f32)],
        [
            pltpu.VMEM((ROWS, d), f32),
            pltpu.VMEM((ROWS, v), f32),
            pltpu.VMEM((ROWS, v), f32),
            pltpu.VMEM((2 * ROWS, v), f32),
        ],
    )(*pieces, head_weight, own_t, got_t)
    got = lax.ppermute(send, "teach", flip(2, 1))
    stats, keep, send = call(
        second_kernel, [((ROWS, STATS), f32), ((8, d), f32), ((8, d + 2 * STATS), f32)]
    )(keep, stats, got)
    got = lax.ppermute(send, "rows", flip(2, 1))
    stats, keep, *sends = call(
        third_kernel,
        [((ROWS, STATS), f32), ((2, d), f32)] + [((2, d + 8 * STATS), f32)] * 3,
        [pltpu.VMEM((ROWS, STATS), f32)],
    )(keep, stats, got)
    gots = [lax.ppermute(a, "vocab", flip(4, k)) for k, a in enumerate(sends, 1)]
    chunk = 512
    divergence, hidden_grad, weight_grad = call(
        make_last_kernel(chunk),
        [((1, STATS), f32), ((1, d), bf16), ((v, d), bf16)],
        [
            pltpu.VMEM((3, ROWS, STATS), f32),
            pltpu.VMEM((ROWS, d), f32),
            pltpu.VMEM((ROWS, v), f32),
            pltpu.VMEM((v, d), bf16),
            pltpu.SemaphoreType.DMA((d // chunk,)),
        ],
        [SMEM] + [VMEM] * 11,
        [VMEM, VMEM, pl.BlockSpec(memory_space=pl.ANY)],
    )(row_mask, keep, stats, *gots, student, scaled, *pieces)
    return divergence[0, :ROWS], hidden_grad, weight_grad


def solution(mesh):
    sizes = mesh.shape["vocab"], mesh.shape["rows"], mesh.shape["teach"]
    general = make_body(*sizes)

    def body(hidden_rows, mentor, head_weight, row_mask):
        small = sizes == (4, 2, 2) and row_mask.shape[0] == ROWS and head_weight.shape[1] % 512 == 0
        return (small_body if small else general)(hidden_rows, mentor, head_weight, row_mask)
    return jax.shard_map(
        body,
        mesh=mesh,
        in_specs=(
            P(("groups", "vocab"), None),
            P(("groups", "teach"), ("vocab", "rows")),
            P(("vocab", "rows", "teach"), None),
            P("groups"),
        ),
        out_specs=(
            P("groups"),
            P(("groups", "vocab", "rows", "teach"), None),
            P(("groups", "vocab", "rows", "teach"), None),
        ),
        check_vma=False,
    )
```

```python
import jax
import jax.numpy as jnp
from jax import lax
from jax.experimental import pallas as pl
from jax.experimental.pallas import tpu as pltpu
from jax.sharding import PartitionSpec as P

smoothing_divisor = 2.0
objective_scale = 256.0


def flip(n, d):
    return [(i, i ^ d) for i in range(n)]


def bits(n):
    out = []
    d = 1
    while d < n:
        out.append(d)
        d *= 2
    return out


def swap(a, d):
    n = a.shape[0]
    b = a.reshape((n // (2 * d), 2, d) + a.shape[1:])
    return jnp.concatenate([b[:, 1:], b[:, :1]], axis=1).reshape(a.shape)


def relative(a, position, n, stride):
    for d in bits(n):
        a = jnp.where((position & d) != 0, swap(a, d * stride), a)
    return a


def make_body(nz, nx, nc):
    def body(hidden_rows, mentor, head_weight, row_mask):
        z, x, c = lax.axis_index("vocab"), lax.axis_index("rows"), lax.axis_index("teach")
        total = row_mask.shape[0]
        q = total // (nz * nx * nc)
        own = relative(relative(hidden_rows, c, nc, q), x, nx, q * nc)
        gathered = own
        if nz == 4:
            gathered = jnp.concatenate(
                [own] + [lax.ppermute(own, "vocab", flip(nz, k)) for k in (1, 2, 3)], 0
            )
        else:
            for d in bits(nz):
                gathered = jnp.concatenate([gathered, lax.ppermute(gathered, "vocab", flip(nz, d))], 0)
        width = mentor.shape[1] // 2
        left, right = mentor[:, :width], mentor[:, width:]
        kept = jnp.where(c == 0, left, right)
        got = lax.ppermute(jnp.where(c == 0, right, left), "teach", flip(nc, 1))
        scaled = jnp.concatenate([jnp.where(c == 0, kept, got), jnp.where(c == 0, got, kept)], 0)

        def rel(a):
            a = relative(a, c, nc, q)
            a = relative(a, x, nx, q * nc)
            return relative(a, z, nz, q * nc * nx)

        scaled = rel(scaled) / smoothing_divisor
        mask = rel(row_mask).astype(jnp.float32)
        student = (
            lax.dot_general(
                gathered, head_weight, (((1,), (1,)), ((), ())), preferred_element_type=jnp.float32
            )
            / smoothing_divisor
        )
        ms = jnp.max(student, axis=1)
        mt = jnp.max(scaled, axis=1)
        es = jnp.exp(student - ms[:, None])
        et = jnp.exp(scaled - mt[:, None])
        stats = jnp.stack(
            [ms, mt, jnp.sum(es, axis=1), jnp.sum(et, axis=1), jnp.sum(et * (scaled - student), axis=1)], 0
        )
        both = jnp.concatenate([es, et], 0)
        high = both.astype(jnp.bfloat16)
        low = (both - high.astype(jnp.float32)).astype(jnp.bfloat16)
        part = jnp.dot(
            jnp.concatenate([high, low], 0), head_weight, preferred_element_type=jnp.float32
        )
        part = part[: 2 * total] + part[2 * total :]
        part = part.reshape(2, nz, nx, nc, q, -1)

        def merge(keep, stats, others):
            top = stats[:2]
            for _, s in others:
                top = jnp.maximum(top, s[:2])
            factor = [jnp.exp(s[:2] - top) for s in [stats] + [s for _, s in others]]
            sums = sum(
                jnp.concatenate([f * s[2:4], (f[1] * s[4])[None]], 0)
                for f, s in zip(factor, [stats] + [s for _, s in others])
            )
            return top, factor, jnp.concatenate([top, sums], 0)

        def level(part, stats, axis, n, dim, stride):
            if n == 4:
                steps = [(1, 2, 3)]
            else:
                steps = [(d,) for d in reversed(bits(n))]
            size = n
            for ds in steps:
                span = size // (len(ds) + 1)
                keep = lax.slice_in_dim(part, 0, span, axis=dim)
                others = []
                for d in ds:
                    a = lax.ppermute(lax.slice_in_dim(part, d, d + span, axis=dim), axis, flip(n, d))
                    s = lax.ppermute(stats, axis, flip(n, d))
                    s = s.T
                    for b in bits(n):
                        if d & b:
                            s = swap(s, b * stride)
                    others.append((a, s.T))
                _, factor, stats = merge(keep, stats, others)
                rows = [f.reshape(2, nz, nx, nc, q, 1) for f in factor]

                def cut(f):
                    shape = keep.shape
                    for ax in range(1, 4):
                        f = lax.slice_in_dim(f, 0, shape[ax], axis=ax)
                    return f

                part = keep * cut(rows[0])
                for (a, _), f in zip(others, rows[1:]):
                    part = part + a * cut(f)
                size = span
            return part, stats

        part, stats = level(part, stats, "teach", nc, 3, q)
        part, stats = level(part, stats, "rows", nx, 2, q * nc)
        part, stats = level(part, stats, "vocab", nz, 1, q * nc * nx)
        part = part.reshape(2, q, -1)
        ms, mt, ls, lt, cross = stats
        lse_s = ms + jnp.log(ls)
        lse_t = mt + jnp.log(lt)
        divergence = rel(mask * (cross / lt - lse_t + lse_s))
        gain = mask * (objective_scale * smoothing_divisor)
        grad = (
            gain[:, None] * (jnp.exp(student - lse_s[:, None]) - jnp.exp(scaled - lse_t[:, None]))
        ).astype(jnp.bfloat16)
        weight_grad = lax.dot_general(
            grad, gathered, (((0,), (0,)), ((), ())), preferred_element_type=jnp.float32
        )
        hidden_grad = gain[:q, None] * (part[0] / ls[:q, None] - part[1] / lt[:q, None])
        return divergence, hidden_grad.astype(jnp.bfloat16), weight_grad.astype(jnp.bfloat16)

    return body


ROWS = 16
STATS = 128


def pack(columns):
    lane = lax.broadcasted_iota(jnp.int32, (ROWS, STATS), 1)
    out = jnp.zeros((ROWS, STATS), jnp.float32)
    for i, column in enumerate(columns):
        out = jnp.where(lane == i, column, out)
    return out


def unite(parts):
    top = parts[0]
    for s in parts[1:]:
        top = jnp.maximum(top, s)
    factors = [jnp.exp(s - top) for s in parts]
    ls = sum(s[:, 2:3] * f[:, 0:1] for s, f in zip(parts, factors))
    lt = sum(s[:, 3:4] * f[:, 1:2] for s, f in zip(parts, factors))
    cross = sum(s[:, 4:5] * f[:, 1:2] for s, f in zip(parts, factors))
    return factors, [top[:, 0:1], top[:, 1:2], ls, lt, cross, top[:, 5:6]]


def places():
    return lax.axis_index("vocab"), lax.axis_index("rows"), lax.axis_index("teach")


def row_of(b, x, c):
    return 2 * (x ^ (b & 1)) + (c ^ (b >> 1))


def teacher_kernel(mask_in, own_in, got, h, scaled, et, stats, h_out, tt, mask, own, sems):
    copies = [
        pltpu.make_async_copy(a, b, sems.at[i])
        for i, (a, b) in enumerate(((own_in, own), (mask_in, mask), (h, h_out)))
    ]
    for copy in copies:
        copy.start()
    z, x, c = places()
    v = scaled.shape[1]
    copies[0].wait()
    copies[1].wait()
    for i, tile in ((c, own[...]), (1 - c, got[...])):
        tt[pl.ds(pl.multiple_of(8 * i, 8), 8), :] = 0.5 * jnp.where(c == 0, tile[:, 0:v], tile[:, v : 2 * v])
    row = lax.broadcasted_iota(jnp.int32, (ROWS, 1), 0)
    valid = jnp.zeros((ROWS, 1), jnp.float32)
    for r in range(ROWS):
        at = 4 * ((r & 3) ^ z) + row_of(r >> 2, x, c)
        scaled[r : r + 1, :] = tt[pl.ds(at, 1), :]
        valid = jnp.where(row == r, mask[at].astype(jnp.float32), valid)
    t = scaled[...]
    mt = jnp.max(t, axis=1, keepdims=True)
    e = jnp.exp(t - mt)
    et[...] = e
    none = jnp.zeros_like(mt)
    stats[...] = pack([none, mt, none, jnp.sum(e, axis=1, keepdims=True), none, valid])
    copies[2].wait()


def first_kernel(h0, h1, h2, h3, w, scaled, et_in, teacher, student, stats, hb, keep, send, hf, raw, e):
    z, x, c = places()
    for k, h in enumerate((h0, h1, h2, h3)):
        hf[4 * k : 4 * k + 4, :] = h[...].astype(jnp.float32)
    rows = hf[...].astype(jnp.bfloat16)
    hb[...] = rows
    raw[...] = 0.5 * lax.dot_general(
        rows, w[...], (((1,), (1,)), ((), ())), preferred_element_type=jnp.float32
    )
    for b in range(4):
        j = row_of(b, x, c)
        for k in range(4):
            student[4 * b + k : 4 * b + k + 1, :] = raw[pl.ds(4 * k + j, 1), :]
    s = student[...]
    t = scaled[...]
    et = et_in[...]
    ms = jnp.max(s, axis=1, keepdims=True)
    es = jnp.exp(s - ms)
    st = pack(
        [
            ms,
            teacher[:, 1:2],
            jnp.sum(es, axis=1, keepdims=True),
            teacher[:, 3:4],
            jnp.sum(et * (t - s), axis=1, keepdims=True),
            teacher[:, 5:6],
        ]
    )
    stats[...] = st
    for b in range(4):
        e[8 * b : 8 * b + 4, :] = es[4 * b : 4 * b + 4, :]
        e[8 * b + 4 : 8 * b + 8, :] = et[4 * b : 4 * b + 4, :]
    both = e[...]
    high = both.astype(jnp.bfloat16)
    low = (both - high.astype(jnp.float32)).astype(jnp.bfloat16)
    part = jnp.dot(jnp.concatenate([high, low], 0), w[...], preferred_element_type=jnp.float32)
    d = part.shape[1]
    keep[...] = part[0:16] + part[32:48]
    send[:, 0:d] = part[16:32] + part[48:64]
    send[0:8, d:] = st[8:16]
    send[8:16, d:] = st[0:8]


def second_kernel(part, stats, got, stats_out, keep, send):
    d = part.shape[1]
    factors, columns = unite([stats[...], got[:, d:]])
    st = pack(columns)
    stats_out[...] = st
    scale = [
        jnp.concatenate([f[0:4, 0:1], f[0:4, 1:2], f[4:8, 0:1], f[4:8, 1:2]], 0) for f in factors
    ]
    total = part[...] * scale[0] + got[:, 0:d] * scale[1]
    keep[...] = total[0:8]
    send[:, 0:d] = total[8:16]
    for i in range(2):
        send[0:4, d + 128 * i : d + 128 * i + 128] = st[8 * i + 4 : 8 * i + 8]
        send[4:8, d + 128 * i : d + 128 * i + 128] = st[8 * i : 8 * i + 4]


def third_kernel(part, stats, got, stats_out, keep, send1, send2, send3, gs):
    d = part.shape[1]
    for i in range(2):
        gs[8 * i : 8 * i + 8, :] = got[:, d + 128 * i : d + 128 * i + 128]
    factors, columns = unite([stats[...], gs[...]])
    st = pack(columns)
    stats_out[...] = st
    scale = [jnp.concatenate([f[0:4, 0:1], f[0:4, 1:2]], 0) for f in factors]
    total = part[...] * scale[0] + got[:, 0:d] * scale[1]
    keep[0:1, :] = total[0:1]
    keep[1:2, :] = total[4:5]
    for k, send in enumerate((send1, send2, send3), 1):
        send[0:1, 0:d] = total[k : k + 1]
        send[1:2, 0:d] = total[4 + k : 5 + k]
        for p in range(ROWS):
            at = d + 128 * (p // 2)
            r = p ^ k
            send[p % 2 : p % 2 + 1, at : at + 128] = st[r : r + 1]


def make_last_kernel(chunk):
    def last_kernel(
        part, stats, got1, got2, got3, student, scaled, hb,
        divergence, hidden_grad, weight_grad, gs, gr, out, sems,
    ):
        z, x, c = places()
        d = part.shape[1]
        parts = [stats[...]]
        for k, got in enumerate((got1, got2, got3)):
            for i in range(8):
                gs[k, 2 * i : 2 * i + 2, :] = got[:, d + 128 * i : d + 128 * i + 128]
            parts.append(gs[k])
        factors, (ms, mt, ls, lt, cross, valid) = unite(parts)
        lse_s = ms + jnp.log(ls)
        lse_t = mt + jnp.log(lt)
        gain = valid * (objective_scale * smoothing_divisor)
        grad = gain * (jnp.exp(student[...] - lse_s) - jnp.exp(scaled[...] - lse_t))
        for b in range(4):
            j = row_of(b, x, c)
            for k in range(4):
                gr[pl.ds(4 * k + j, 1), :] = grad[4 * b + k : 4 * b + k + 1, :]
        g = gr[...].astype(jnp.bfloat16)
        copies = []
        for i in range(d // chunk):
            at = pl.ds(i * chunk, chunk)
            out[:, at] = lax.dot_general(
                g, hb[:, at], (((0,), (0,)), ((), ())), preferred_element_type=jnp.float32
            ).astype(jnp.bfloat16)
            copy = pltpu.make_async_copy(out.at[:, at], weight_grad.at[:, at], sems.at[i])
            copy.start()
            copies.append(copy)
        row = lax.broadcasted_iota(jnp.int32, (ROWS, 1), 0)
        home = 4 * (z ^ (row & 3)) + 2 * (x ^ ((row >> 2) & 1)) + (c ^ (row >> 3))
        value = valid * (cross / lt - lse_t + lse_s)
        lane = lax.broadcasted_iota(jnp.int32, (ROWS, STATS), 1)
        divergence[...] = jnp.sum(jnp.where(lane == home, value, 0.0), axis=0)[0:ROWS]
        a_s = part[0:1, :] * factors[0][0:1, 0:1]
        a_t = part[1:2, :] * factors[0][0:1, 1:2]
        for got, f in zip((got1, got2, got3), factors[1:]):
            a_s = a_s + got[0:1, 0:d] * f[0:1, 0:1]
            a_t = a_t + got[1:2, 0:d] * f[0:1, 1:2]
        hidden_grad[...] = (
            gain[0:1] * (a_s / ls[0:1] - a_t / lt[0:1])
        ).astype(jnp.bfloat16)
        for copy in copies:
            copy.wait()

    return last_kernel


VMEM = pl.BlockSpec(memory_space=pltpu.VMEM)
ANY = pl.BlockSpec(memory_space=pl.ANY)
PARAMS = pltpu.CompilerParams(vmem_limit_bytes=32 << 20)


def call(kernel, out, scratch=(), in_specs=None, out_specs=None, cost=None):
    shapes = [jax.ShapeDtypeStruct(s, t) for s, t in out]
    return lambda *a: pl.pallas_call(
        kernel,
        out_shape=shapes,
        in_specs=in_specs or [VMEM] * len(a),
        out_specs=out_specs or [VMEM] * len(out),
        scratch_shapes=list(scratch),
        compiler_params=PARAMS,
        cost_estimate=cost,
    )(*a)


def small_body(hidden_rows, mentor, head_weight, row_mask):
    f32, bf16 = jnp.float32, jnp.bfloat16
    v, d = head_weight.shape
    pieces = [lax.ppermute(hidden_rows, "vocab", flip(4, k)) for k in (1, 2, 3)]
    scaled, et, teacher, own = call(
        teacher_kernel,
        [((ROWS, v), f32), ((ROWS, v), f32), ((ROWS, STATS), f32), ((4, d), bf16)],
        [
            pltpu.VMEM((ROWS, v), f32),
            pltpu.SMEM((ROWS,), jnp.int32),
            pltpu.VMEM((ROWS // 2, 2 * v), f32),
            pltpu.SemaphoreType.DMA((3,)),
        ],
        [ANY, ANY, VMEM, ANY],
        cost=pl.CostEstimate(flops=2_000_000_000, transcendentals=ROWS * v, bytes_accessed=2 << 20),
    )(row_mask, mentor, lax.ppermute(mentor, "teach", flip(2, 1)), hidden_rows)
    student, stats, hb, keep, send = call(
        first_kernel,
        [((ROWS, v), f32), ((ROWS, STATS), f32), ((ROWS, d), bf16), ((16, d), f32), ((16, d + STATS), f32)],
        [
            pltpu.VMEM((ROWS, d), f32),
            pltpu.VMEM((ROWS, v), f32),
            pltpu.VMEM((2 * ROWS, v), f32),
        ],
    )(own, *pieces, head_weight, scaled, et, teacher)
    got = lax.ppermute(send, "teach", flip(2, 1))
    stats, keep, send = call(
        second_kernel, [((ROWS, STATS), f32), ((8, d), f32), ((8, d + 2 * STATS), f32)]
    )(keep, stats, got)
    got = lax.ppermute(send, "rows", flip(2, 1))
    stats, keep, *sends = call(
        third_kernel,
        [((ROWS, STATS), f32), ((2, d), f32)] + [((2, d + 8 * STATS), f32)] * 3,
        [pltpu.VMEM((ROWS, STATS), f32)],
    )(keep, stats, got)
    gots = [lax.ppermute(a, "vocab", flip(4, k)) for k, a in enumerate(sends, 1)]
    chunk = 512
    return tuple(
        call(
            make_last_kernel(chunk),
            [((ROWS,), f32), ((1, d), bf16), ((v, d), bf16)],
            [
                pltpu.VMEM((3, ROWS, STATS), f32),
                pltpu.VMEM((ROWS, v), f32),
                pltpu.VMEM((v, d), bf16),
                pltpu.SemaphoreType.DMA((d // chunk,)),
            ],
            [VMEM] * 8,
            [VMEM, VMEM, ANY],
        )(keep, stats, *gots, student, scaled, hb)
    )


def solution(mesh):
    sizes = mesh.shape["vocab"], mesh.shape["rows"], mesh.shape["teach"]
    general = make_body(*sizes)

    def body(hidden_rows, mentor, head_weight, row_mask):
        small = sizes == (4, 2, 2) and row_mask.shape[0] == ROWS and head_weight.shape[1] % 512 == 0
        return (small_body if small else general)(hidden_rows, mentor, head_weight, row_mask)
    return jax.shard_map(
        body,
        mesh=mesh,
        in_specs=(
            P(("groups", "vocab"), None),
            P(("groups", "teach"), ("vocab", "rows")),
            P(("vocab", "rows", "teach"), None),
            P("groups"),
        ),
        out_specs=(
            P("groups"),
            P(("groups", "vocab", "rows", "teach"), None),
            P(("groups", "vocab", "rows", "teach"), None),
        ),
        check_vma=False,
    )
```

```python
import jax
import jax.numpy as jnp
from jax import lax
from jax.experimental import pallas as pl
from jax.experimental.pallas import tpu as pltpu
from jax.sharding import PartitionSpec as P

smoothing_divisor = 2.0
objective_scale = 256.0


def flip(n, d):
    return [(i, i ^ d) for i in range(n)]


def bits(n):
    out = []
    d = 1
    while d < n:
        out.append(d)
        d *= 2
    return out


def swap(a, d):
    n = a.shape[0]
    b = a.reshape((n // (2 * d), 2, d) + a.shape[1:])
    return jnp.concatenate([b[:, 1:], b[:, :1]], axis=1).reshape(a.shape)


def relative(a, position, n, stride):
    for d in bits(n):
        a = jnp.where((position & d) != 0, swap(a, d * stride), a)
    return a


def make_body(nz, nx, nc):
    def body(hidden_rows, mentor, head_weight, row_mask):
        z, x, c = lax.axis_index("vocab"), lax.axis_index("rows"), lax.axis_index("teach")
        total = row_mask.shape[0]
        q = total // (nz * nx * nc)
        own = relative(relative(hidden_rows, c, nc, q), x, nx, q * nc)
        gathered = own
        if nz == 4:
            gathered = jnp.concatenate(
                [own] + [lax.ppermute(own, "vocab", flip(nz, k)) for k in (1, 2, 3)], 0
            )
        else:
            for d in bits(nz):
                gathered = jnp.concatenate([gathered, lax.ppermute(gathered, "vocab", flip(nz, d))], 0)
        width = mentor.shape[1] // 2
        left, right = mentor[:, :width], mentor[:, width:]
        kept = jnp.where(c == 0, left, right)
        got = lax.ppermute(jnp.where(c == 0, right, left), "teach", flip(nc, 1))
        scaled = jnp.concatenate([jnp.where(c == 0, kept, got), jnp.where(c == 0, got, kept)], 0)

        def rel(a):
            a = relative(a, c, nc, q)
            a = relative(a, x, nx, q * nc)
            return relative(a, z, nz, q * nc * nx)

        scaled = rel(scaled) / smoothing_divisor
        mask = rel(row_mask).astype(jnp.float32)
        student = (
            lax.dot_general(
                gathered, head_weight, (((1,), (1,)), ((), ())), preferred_element_type=jnp.float32
            )
            / smoothing_divisor
        )
        ms = jnp.max(student, axis=1)
        mt = jnp.max(scaled, axis=1)
        es = jnp.exp(student - ms[:, None])
        et = jnp.exp(scaled - mt[:, None])
        stats = jnp.stack(
            [ms, mt, jnp.sum(es, axis=1), jnp.sum(et, axis=1), jnp.sum(et * (scaled - student), axis=1)], 0
        )
        both = jnp.concatenate([es, et], 0)
        high = both.astype(jnp.bfloat16)
        low = (both - high.astype(jnp.float32)).astype(jnp.bfloat16)
        part = jnp.dot(
            jnp.concatenate([high, low], 0), head_weight, preferred_element_type=jnp.float32
        )
        part = part[: 2 * total] + part[2 * total :]
        part = part.reshape(2, nz, nx, nc, q, -1)

        def merge(keep, stats, others):
            top = stats[:2]
            for _, s in others:
                top = jnp.maximum(top, s[:2])
            factor = [jnp.exp(s[:2] - top) for s in [stats] + [s for _, s in others]]
            sums = sum(
                jnp.concatenate([f * s[2:4], (f[1] * s[4])[None]], 0)
                for f, s in zip(factor, [stats] + [s for _, s in others])
            )
            return top, factor, jnp.concatenate([top, sums], 0)

        def level(part, stats, axis, n, dim, stride):
            if n == 4:
                steps = [(1, 2, 3)]
            else:
                steps = [(d,) for d in reversed(bits(n))]
            size = n
            for ds in steps:
                span = size // (len(ds) + 1)
                keep = lax.slice_in_dim(part, 0, span, axis=dim)
                others = []
                for d in ds:
                    a = lax.ppermute(lax.slice_in_dim(part, d, d + span, axis=dim), axis, flip(n, d))
                    s = lax.ppermute(stats, axis, flip(n, d))
                    s = s.T
                    for b in bits(n):
                        if d & b:
                            s = swap(s, b * stride)
                    others.append((a, s.T))
                _, factor, stats = merge(keep, stats, others)
                rows = [f.reshape(2, nz, nx, nc, q, 1) for f in factor]

                def cut(f):
                    shape = keep.shape
                    for ax in range(1, 4):
                        f = lax.slice_in_dim(f, 0, shape[ax], axis=ax)
                    return f

                part = keep * cut(rows[0])
                for (a, _), f in zip(others, rows[1:]):
                    part = part + a * cut(f)
                size = span
            return part, stats

        part, stats = level(part, stats, "teach", nc, 3, q)
        part, stats = level(part, stats, "rows", nx, 2, q * nc)
        part, stats = level(part, stats, "vocab", nz, 1, q * nc * nx)
        part = part.reshape(2, q, -1)
        ms, mt, ls, lt, cross = stats
        lse_s = ms + jnp.log(ls)
        lse_t = mt + jnp.log(lt)
        divergence = rel(mask * (cross / lt - lse_t + lse_s))
        gain = mask * (objective_scale * smoothing_divisor)
        grad = (
            gain[:, None] * (jnp.exp(student - lse_s[:, None]) - jnp.exp(scaled - lse_t[:, None]))
        ).astype(jnp.bfloat16)
        weight_grad = lax.dot_general(
            grad, gathered, (((0,), (0,)), ((), ())), preferred_element_type=jnp.float32
        )
        hidden_grad = gain[:q, None] * (part[0] / ls[:q, None] - part[1] / lt[:q, None])
        return divergence, hidden_grad.astype(jnp.bfloat16), weight_grad.astype(jnp.bfloat16)

    return body


ROWS = 16
STATS = 128


def pack(columns):
    lane = lax.broadcasted_iota(jnp.int32, (ROWS, STATS), 1)
    out = jnp.zeros((ROWS, STATS), jnp.float32)
    for i, column in enumerate(columns):
        out = jnp.where(lane == i, column, out)
    return out


def unite(parts):
    top = parts[0]
    for s in parts[1:]:
        top = jnp.maximum(top, s)
    factors = [jnp.exp(s - top) for s in parts]
    ls = sum(s[:, 2:3] * f[:, 0:1] for s, f in zip(parts, factors))
    lt = sum(s[:, 3:4] * f[:, 1:2] for s, f in zip(parts, factors))
    cross = sum(s[:, 4:5] * f[:, 1:2] for s, f in zip(parts, factors))
    return factors, [top[:, 0:1], top[:, 1:2], ls, lt, cross, top[:, 5:6]]


def places():
    return lax.axis_index("vocab"), lax.axis_index("rows"), lax.axis_index("teach")


def row_of(b, x, c):
    return 2 * (x ^ (b & 1)) + (c ^ (b >> 1))


def teacher_kernel(mask_in, own_in, got, h, scaled, et, stats, h_out, tt, mask, own, sems):
    copies = [
        pltpu.make_async_copy(a, b, sems.at[i])
        for i, (a, b) in enumerate(((own_in, own), (mask_in, mask), (h, h_out)))
    ]
    for copy in copies:
        copy.start()
    z, x, c = places()
    v = scaled.shape[1]
    copies[0].wait()
    copies[1].wait()
    for i, tile in ((c, own[...]), (1 - c, got[...])):
        tt[pl.ds(pl.multiple_of(8 * i, 8), 8), :] = 0.5 * jnp.where(c == 0, tile[:, 0:v], tile[:, v : 2 * v])
    row = lax.broadcasted_iota(jnp.int32, (ROWS, 1), 0)
    valid = jnp.zeros((ROWS, 1), jnp.float32)
    for r in range(ROWS):
        at = 4 * ((r & 3) ^ z) + row_of(r >> 2, x, c)
        scaled[r : r + 1, :] = tt[pl.ds(at, 1), :]
        valid = jnp.where(row == r, mask[at].astype(jnp.float32), valid)
    t = scaled[...]
    mt = jnp.max(t, axis=1, keepdims=True)
    e = jnp.exp(t - mt)
    et[...] = e
    none = jnp.zeros_like(mt)
    stats[...] = pack([none, mt, none, jnp.sum(e, axis=1, keepdims=True), none, valid])
    copies[2].wait()


def first_kernel(h0, h1, h2, h3, w, scaled, et_in, teacher, student, stats, hb, keep, send, hf, raw, e):
    z, x, c = places()
    for k, h in enumerate((h0, h1, h2, h3)):
        hf[4 * k : 4 * k + 4, :] = h[...].astype(jnp.float32)
    rows = hf[...].astype(jnp.bfloat16)
    hb[...] = rows
    raw[...] = 0.5 * lax.dot_general(
        rows, w[...], (((1,), (1,)), ((), ())), preferred_element_type=jnp.float32
    )
    for b in range(4):
        j = row_of(b, x, c)
        for k in range(4):
            student[4 * b + k : 4 * b + k + 1, :] = raw[pl.ds(4 * k + j, 1), :]
    s = student[...]
    t = scaled[...]
    et = et_in[...]
    ms = jnp.max(s, axis=1, keepdims=True)
    es = jnp.exp(s - ms)
    st = pack(
        [
            ms,
            teacher[:, 1:2],
            jnp.sum(es, axis=1, keepdims=True),
            teacher[:, 3:4],
            jnp.sum(et * (t - s), axis=1, keepdims=True),
            teacher[:, 5:6],
        ]
    )
    stats[...] = st
    for b in range(4):
        e[8 * b : 8 * b + 4, :] = es[4 * b : 4 * b + 4, :]
        e[8 * b + 4 : 8 * b + 8, :] = et[4 * b : 4 * b + 4, :]
    both = e[...]
    high = both.astype(jnp.bfloat16)
    low = (both - high.astype(jnp.float32)).astype(jnp.bfloat16)
    part = jnp.dot(jnp.concatenate([high, low], 0), w[...], preferred_element_type=jnp.float32)
    d = part.shape[1]
    keep[...] = part[0:16] + part[32:48]
    send[:, 0:d] = part[16:32] + part[48:64]
    send[0:8, d:] = st[8:16]
    send[8:16, d:] = st[0:8]


def second_kernel(part, stats, got, stats_out, keep, send):
    d = part.shape[1]
    factors, columns = unite([stats[...], got[:, d:]])
    st = pack(columns)
    stats_out[...] = st
    scale = [
        jnp.concatenate([f[0:4, 0:1], f[0:4, 1:2], f[4:8, 0:1], f[4:8, 1:2]], 0) for f in factors
    ]
    total = part[...] * scale[0] + got[:, 0:d] * scale[1]
    keep[...] = total[0:8]
    send[:, 0:d] = total[8:16]
    for i in range(2):
        send[0:4, d + 128 * i : d + 128 * i + 128] = st[8 * i + 4 : 8 * i + 8]
        send[4:8, d + 128 * i : d + 128 * i + 128] = st[8 * i : 8 * i + 4]


def third_kernel(part, stats, got, stats_out, keep, send1, send2, send3, gs):
    d = part.shape[1]
    for i in range(2):
        gs[8 * i : 8 * i + 8, :] = got[:, d + 128 * i : d + 128 * i + 128]
    factors, columns = unite([stats[...], gs[...]])
    st = pack(columns)
    stats_out[...] = st
    scale = [jnp.concatenate([f[0:4, 0:1], f[0:4, 1:2]], 0) for f in factors]
    total = part[...] * scale[0] + got[:, 0:d] * scale[1]
    keep[0:1, :] = total[0:1]
    keep[1:2, :] = total[4:5]
    for k, send in enumerate((send1, send2, send3), 1):
        send[0:1, 0:d] = total[k : k + 1]
        send[1:2, 0:d] = total[4 + k : 5 + k]
        for p in range(ROWS):
            at = d + 128 * (p // 2)
            r = p ^ k
            send[p % 2 : p % 2 + 1, at : at + 128] = st[r : r + 1]


def make_last_kernel(chunk):
    def last_kernel(
        part, stats, got1, got2, got3, student, scaled, hb,
        divergence, hidden_grad, weight_grad, gs, gr, out, sems,
    ):
        z, x, c = places()
        d = part.shape[1]
        parts = [stats[...]]
        for k, got in enumerate((got1, got2, got3)):
            for i in range(8):
                gs[k, 2 * i : 2 * i + 2, :] = got[:, d + 128 * i : d + 128 * i + 128]
            parts.append(gs[k])
        factors, (ms, mt, ls, lt, cross, valid) = unite(parts)
        lse_s = ms + jnp.log(ls)
        lse_t = mt + jnp.log(lt)
        gain = valid * (objective_scale * smoothing_divisor)
        grad = gain * (jnp.exp(student[...] - lse_s) - jnp.exp(scaled[...] - lse_t))
        for b in range(4):
            j = row_of(b, x, c)
            for k in range(4):
                gr[pl.ds(4 * k + j, 1), :] = grad[4 * b + k : 4 * b + k + 1, :]
        g = gr[...].astype(jnp.bfloat16)
        copies = []
        for i in range(d // chunk):
            at = pl.ds(i * chunk, chunk)
            out[:, at] = lax.dot_general(
                g, hb[:, at], (((0,), (0,)), ((), ())), preferred_element_type=jnp.float32
            ).astype(jnp.bfloat16)
            copy = pltpu.make_async_copy(out.at[:, at], weight_grad.at[:, at], sems.at[i])
            copy.start()
            copies.append(copy)
        row = lax.broadcasted_iota(jnp.int32, (ROWS, 1), 0)
        home = 4 * (z ^ (row & 3)) + 2 * (x ^ ((row >> 2) & 1)) + (c ^ (row >> 3))
        value = valid * (cross / lt - lse_t + lse_s)
        lane = lax.broadcasted_iota(jnp.int32, (ROWS, STATS), 1)
        divergence[...] = jnp.sum(jnp.where(lane == home, value, 0.0), axis=0)[0:ROWS]
        a_s = part[0:1, :] * factors[0][0:1, 0:1]
        a_t = part[1:2, :] * factors[0][0:1, 1:2]
        for got, f in zip((got1, got2, got3), factors[1:]):
            a_s = a_s + got[0:1, 0:d] * f[0:1, 0:1]
            a_t = a_t + got[1:2, 0:d] * f[0:1, 1:2]
        hidden_grad[...] = (
            gain[0:1] * (a_s / ls[0:1] - a_t / lt[0:1])
        ).astype(jnp.bfloat16)
        for copy in copies:
            copy.wait()

    return last_kernel


VMEM = pl.BlockSpec(memory_space=pltpu.VMEM)
ANY = pl.BlockSpec(memory_space=pltpu.HBM)
PARAMS = pltpu.CompilerParams(vmem_limit_bytes=32 << 20)


def call(kernel, out, scratch=(), in_specs=None, out_specs=None, cost=None):
    shapes = [jax.ShapeDtypeStruct(s, t) for s, t in out]
    return lambda *a: pl.pallas_call(
        kernel,
        out_shape=shapes,
        in_specs=in_specs or [VMEM] * len(a),
        out_specs=out_specs or [VMEM] * len(out),
        scratch_shapes=list(scratch),
        compiler_params=PARAMS,
        cost_estimate=cost,
    )(*a)


def small_body(hidden_rows, mentor, head_weight, row_mask):
    f32, bf16 = jnp.float32, jnp.bfloat16
    v, d = head_weight.shape
    pieces = [lax.ppermute(hidden_rows, "vocab", flip(4, k)) for k in (1, 2, 3)]
    scaled, et, teacher, own = call(
        teacher_kernel,
        [((ROWS, v), f32), ((ROWS, v), f32), ((ROWS, STATS), f32), ((4, d), bf16)],
        [
            pltpu.VMEM((ROWS, v), f32),
            pltpu.SMEM((ROWS,), jnp.int32),
            pltpu.VMEM((ROWS // 2, 2 * v), f32),
            pltpu.SemaphoreType.DMA((3,)),
        ],
        [ANY, ANY, VMEM, ANY],
        cost=pl.CostEstimate(flops=2_000_000_000, transcendentals=ROWS * v, bytes_accessed=2 << 20),
    )(
        pltpu.with_memory_space_constraint(row_mask, pltpu.HBM),
        pltpu.with_memory_space_constraint(mentor, pltpu.HBM),
        lax.ppermute(mentor, "teach", flip(2, 1)),
        pltpu.with_memory_space_constraint(hidden_rows, pltpu.HBM),
    )
    student, stats, hb, keep, send = call(
        first_kernel,
        [((ROWS, v), f32), ((ROWS, STATS), f32), ((ROWS, d), bf16), ((16, d), f32), ((16, d + STATS), f32)],
        [
            pltpu.VMEM((ROWS, d), f32),
            pltpu.VMEM((ROWS, v), f32),
            pltpu.VMEM((2 * ROWS, v), f32),
        ],
    )(own, *pieces, head_weight, scaled, et, teacher)
    got = lax.ppermute(send, "teach", flip(2, 1))
    stats, keep, send = call(
        second_kernel, [((ROWS, STATS), f32), ((8, d), f32), ((8, d + 2 * STATS), f32)]
    )(keep, stats, got)
    got = lax.ppermute(send, "rows", flip(2, 1))
    stats, keep, *sends = call(
        third_kernel,
        [((ROWS, STATS), f32), ((2, d), f32)] + [((2, d + 8 * STATS), f32)] * 3,
        [pltpu.VMEM((ROWS, STATS), f32)],
    )(keep, stats, got)
    gots = [lax.ppermute(a, "vocab", flip(4, k)) for k, a in enumerate(sends, 1)]
    chunk = 512
    return tuple(
        call(
            make_last_kernel(chunk),
            [((ROWS,), f32), ((1, d), bf16), ((v, d), bf16)],
            [
                pltpu.VMEM((3, ROWS, STATS), f32),
                pltpu.VMEM((ROWS, v), f32),
                pltpu.VMEM((v, d), bf16),
                pltpu.SemaphoreType.DMA((d // chunk,)),
            ],
            [VMEM] * 8,
            [VMEM, VMEM, ANY],
        )(keep, stats, *gots, student, scaled, hb)
    )


def solution(mesh):
    sizes = mesh.shape["vocab"], mesh.shape["rows"], mesh.shape["teach"]
    general = make_body(*sizes)

    def body(hidden_rows, mentor, head_weight, row_mask):
        small = sizes == (4, 2, 2) and row_mask.shape[0] == ROWS and head_weight.shape[1] % 512 == 0
        return (small_body if small else general)(hidden_rows, mentor, head_weight, row_mask)
    return jax.shard_map(
        body,
        mesh=mesh,
        in_specs=(
            P(("groups", "vocab"), None),
            P(("groups", "teach"), ("vocab", "rows")),
            P(("vocab", "rows", "teach"), None),
            P("groups"),
        ),
        out_specs=(
            P("groups"),
            P(("groups", "vocab", "rows", "teach"), None),
            P(("groups", "vocab", "rows", "teach"), None),
        ),
        check_vma=False,
    )
```

```python
import jax
import jax.numpy as jnp
from jax import lax
from jax.experimental import pallas as pl
from jax.experimental.pallas import tpu as pltpu
from jax.sharding import PartitionSpec as P

smoothing_divisor = 2.0
objective_scale = 256.0


def flip(n, d):
    return [(i, i ^ d) for i in range(n)]


def bits(n):
    out = []
    d = 1
    while d < n:
        out.append(d)
        d *= 2
    return out


def swap(a, d):
    n = a.shape[0]
    b = a.reshape((n // (2 * d), 2, d) + a.shape[1:])
    return jnp.concatenate([b[:, 1:], b[:, :1]], axis=1).reshape(a.shape)


def relative(a, position, n, stride):
    for d in bits(n):
        a = jnp.where((position & d) != 0, swap(a, d * stride), a)
    return a


def make_body(nz, nx, nc):
    def body(hidden_rows, mentor, head_weight, row_mask):
        z, x, c = lax.axis_index("vocab"), lax.axis_index("rows"), lax.axis_index("teach")
        total = row_mask.shape[0]
        q = total // (nz * nx * nc)
        own = relative(relative(hidden_rows, c, nc, q), x, nx, q * nc)
        gathered = own
        if nz == 4:
            gathered = jnp.concatenate(
                [own] + [lax.ppermute(own, "vocab", flip(nz, k)) for k in (1, 2, 3)], 0
            )
        else:
            for d in bits(nz):
                gathered = jnp.concatenate([gathered, lax.ppermute(gathered, "vocab", flip(nz, d))], 0)
        width = mentor.shape[1] // 2
        left, right = mentor[:, :width], mentor[:, width:]
        kept = jnp.where(c == 0, left, right)
        got = lax.ppermute(jnp.where(c == 0, right, left), "teach", flip(nc, 1))
        scaled = jnp.concatenate([jnp.where(c == 0, kept, got), jnp.where(c == 0, got, kept)], 0)

        def rel(a):
            a = relative(a, c, nc, q)
            a = relative(a, x, nx, q * nc)
            return relative(a, z, nz, q * nc * nx)

        scaled = rel(scaled) / smoothing_divisor
        mask = rel(row_mask).astype(jnp.float32)
        student = (
            lax.dot_general(
                gathered, head_weight, (((1,), (1,)), ((), ())), preferred_element_type=jnp.float32
            )
            / smoothing_divisor
        )
        ms = jnp.max(student, axis=1)
        mt = jnp.max(scaled, axis=1)
        es = jnp.exp(student - ms[:, None])
        et = jnp.exp(scaled - mt[:, None])
        stats = jnp.stack(
            [ms, mt, jnp.sum(es, axis=1), jnp.sum(et, axis=1), jnp.sum(et * (scaled - student), axis=1)], 0
        )
        both = jnp.concatenate([es, et], 0)
        high = both.astype(jnp.bfloat16)
        low = (both - high.astype(jnp.float32)).astype(jnp.bfloat16)
        part = jnp.dot(
            jnp.concatenate([high, low], 0), head_weight, preferred_element_type=jnp.float32
        )
        part = part[: 2 * total] + part[2 * total :]
        part = part.reshape(2, nz, nx, nc, q, -1)

        def merge(keep, stats, others):
            top = stats[:2]
            for _, s in others:
                top = jnp.maximum(top, s[:2])
            factor = [jnp.exp(s[:2] - top) for s in [stats] + [s for _, s in others]]
            sums = sum(
                jnp.concatenate([f * s[2:4], (f[1] * s[4])[None]], 0)
                for f, s in zip(factor, [stats] + [s for _, s in others])
            )
            return top, factor, jnp.concatenate([top, sums], 0)

        def level(part, stats, axis, n, dim, stride):
            if n == 4:
                steps = [(1, 2, 3)]
            else:
                steps = [(d,) for d in reversed(bits(n))]
            size = n
            for ds in steps:
                span = size // (len(ds) + 1)
                keep = lax.slice_in_dim(part, 0, span, axis=dim)
                others = []
                for d in ds:
                    a = lax.ppermute(lax.slice_in_dim(part, d, d + span, axis=dim), axis, flip(n, d))
                    s = lax.ppermute(stats, axis, flip(n, d))
                    s = s.T
                    for b in bits(n):
                        if d & b:
                            s = swap(s, b * stride)
                    others.append((a, s.T))
                _, factor, stats = merge(keep, stats, others)
                rows = [f.reshape(2, nz, nx, nc, q, 1) for f in factor]

                def cut(f):
                    shape = keep.shape
                    for ax in range(1, 4):
                        f = lax.slice_in_dim(f, 0, shape[ax], axis=ax)
                    return f

                part = keep * cut(rows[0])
                for (a, _), f in zip(others, rows[1:]):
                    part = part + a * cut(f)
                size = span
            return part, stats

        part, stats = level(part, stats, "teach", nc, 3, q)
        part, stats = level(part, stats, "rows", nx, 2, q * nc)
        part, stats = level(part, stats, "vocab", nz, 1, q * nc * nx)
        part = part.reshape(2, q, -1)
        ms, mt, ls, lt, cross = stats
        lse_s = ms + jnp.log(ls)
        lse_t = mt + jnp.log(lt)
        divergence = rel(mask * (cross / lt - lse_t + lse_s))
        gain = mask * (objective_scale * smoothing_divisor)
        grad = (
            gain[:, None] * (jnp.exp(student - lse_s[:, None]) - jnp.exp(scaled - lse_t[:, None]))
        ).astype(jnp.bfloat16)
        weight_grad = lax.dot_general(
            grad, gathered, (((0,), (0,)), ((), ())), preferred_element_type=jnp.float32
        )
        hidden_grad = gain[:q, None] * (part[0] / ls[:q, None] - part[1] / lt[:q, None])
        return divergence, hidden_grad.astype(jnp.bfloat16), weight_grad.astype(jnp.bfloat16)

    return body


ROWS = 16
STATS = 128


def pack(columns):
    lane = lax.broadcasted_iota(jnp.int32, (ROWS, STATS), 1)
    out = jnp.zeros((ROWS, STATS), jnp.float32)
    for i, column in enumerate(columns):
        out = jnp.where(lane == i, column, out)
    return out


def unite(parts):
    top = parts[0]
    for s in parts[1:]:
        top = jnp.maximum(top, s)
    factors = [jnp.exp(s - top) for s in parts]
    ls = sum(s[:, 2:3] * f[:, 0:1] for s, f in zip(parts, factors))
    lt = sum(s[:, 3:4] * f[:, 1:2] for s, f in zip(parts, factors))
    cross = sum(s[:, 4:5] * f[:, 1:2] for s, f in zip(parts, factors))
    return factors, [top[:, 0:1], top[:, 1:2], ls, lt, cross, top[:, 5:6]]


def places():
    return lax.axis_index("vocab"), lax.axis_index("rows"), lax.axis_index("teach")


def row_of(b, x, c):
    return 2 * (x ^ (b & 1)) + (c ^ (b >> 1))


def teacher_kernel(mask_in, own_in, got, h, scaled, et, stats, h_out, tt, mask, own, sems):
    copies = [
        pltpu.make_async_copy(a, b, sems.at[i])
        for i, (a, b) in enumerate(((own_in, own), (mask_in, mask), (h, h_out)))
    ]
    for copy in copies:
        copy.start()
    z, x, c = places()
    v = scaled.shape[1]
    copies[0].wait()
    copies[1].wait()
    for i, tile in ((c, own[...]), (1 - c, got[...])):
        tt[pl.ds(pl.multiple_of(8 * i, 8), 8), :] = 0.5 * jnp.where(c == 0, tile[:, 0:v], tile[:, v : 2 * v])
    row = lax.broadcasted_iota(jnp.int32, (ROWS, 1), 0)
    valid = jnp.zeros((ROWS, 1), jnp.float32)
    for r in range(ROWS):
        at = 4 * ((r & 3) ^ z) + row_of(r >> 2, x, c)
        scaled[r : r + 1, :] = tt[pl.ds(at, 1), :]
        valid = jnp.where(row == r, mask[at].astype(jnp.float32), valid)
    t = scaled[...]
    mt = jnp.max(t, axis=1, keepdims=True)
    e = jnp.exp(t - mt)
    et[...] = e
    none = jnp.zeros_like(mt)
    stats[...] = pack([none, mt, none, jnp.sum(e, axis=1, keepdims=True), none, valid])
    copies[2].wait()


def first_kernel(h0, h1, h2, h3, w, scaled, et_in, teacher, student, stats, hb, keep, send, hf, raw, e):
    z, x, c = places()
    for k, h in enumerate((h0, h1, h2, h3)):
        hf[4 * k : 4 * k + 4, :] = h[...].astype(jnp.float32)
    rows = hf[...].astype(jnp.bfloat16)
    hb[...] = rows
    raw[...] = 0.5 * lax.dot_general(
        rows, w[...], (((1,), (1,)), ((), ())), preferred_element_type=jnp.float32
    )

    @pl.when(z >= 0)
    def _():
        for b in range(4):
            j = row_of(b, x, c)
            for k in range(4):
                student[4 * b + k : 4 * b + k + 1, :] = raw[pl.ds(4 * k + j, 1), :]
        s = student[...]
        t = scaled[...]
        et = et_in[...]
        ms = jnp.max(s, axis=1, keepdims=True)
        es = jnp.exp(s - ms)
        st = pack(
            [
                ms,
                teacher[:, 1:2],
                jnp.sum(es, axis=1, keepdims=True),
                teacher[:, 3:4],
                jnp.sum(et * (t - s), axis=1, keepdims=True),
                teacher[:, 5:6],
            ]
        )
        stats[...] = st
        for b in range(4):
            e[8 * b : 8 * b + 4, :] = es[4 * b : 4 * b + 4, :]
            e[8 * b + 4 : 8 * b + 8, :] = et[4 * b : 4 * b + 4, :]
        both = e[...]
        high = both.astype(jnp.bfloat16)
        low = (both - high.astype(jnp.float32)).astype(jnp.bfloat16)
        part = jnp.dot(jnp.concatenate([high, low], 0), w[...], preferred_element_type=jnp.float32)
        d = part.shape[1]
        keep[...] = part[0:16] + part[32:48]
        send[:, 0:d] = part[16:32] + part[48:64]
        send[0:8, d:] = st[8:16]
        send[8:16, d:] = st[0:8]


def second_kernel(part, stats, got, stats_out, keep, send):
    d = part.shape[1]
    factors, columns = unite([stats[...], got[:, d:]])
    st = pack(columns)
    stats_out[...] = st
    scale = [
        jnp.concatenate([f[0:4, 0:1], f[0:4, 1:2], f[4:8, 0:1], f[4:8, 1:2]], 0) for f in factors
    ]
    total = part[...] * scale[0] + got[:, 0:d] * scale[1]
    keep[...] = total[0:8]
    send[:, 0:d] = total[8:16]
    for i in range(2):
        send[0:4, d + 128 * i : d + 128 * i + 128] = st[8 * i + 4 : 8 * i + 8]
        send[4:8, d + 128 * i : d + 128 * i + 128] = st[8 * i : 8 * i + 4]


def third_kernel(part, stats, got, stats_out, keep, send1, send2, send3, gs):
    d = part.shape[1]
    for i in range(2):
        gs[8 * i : 8 * i + 8, :] = got[:, d + 128 * i : d + 128 * i + 128]
    factors, columns = unite([stats[...], gs[...]])
    st = pack(columns)
    stats_out[...] = st
    scale = [jnp.concatenate([f[0:4, 0:1], f[0:4, 1:2]], 0) for f in factors]
    total = part[...] * scale[0] + got[:, 0:d] * scale[1]
    keep[0:1, :] = total[0:1]
    keep[1:2, :] = total[4:5]
    for k, send in enumerate((send1, send2, send3), 1):
        send[0:1, 0:d] = total[k : k + 1]
        send[1:2, 0:d] = total[4 + k : 5 + k]
        for p in range(ROWS):
            at = d + 128 * (p // 2)
            r = p ^ k
            send[p % 2 : p % 2 + 1, at : at + 128] = st[r : r + 1]


def make_last_kernel(chunk):
    def last_kernel(
        part, stats, got1, got2, got3, student, scaled, hb,
        divergence, hidden_grad, weight_grad, gs, gr, out, div, hid, sems,
    ):
        z, x, c = places()
        d = part.shape[1]
        parts = [stats[...]]
        for k, got in enumerate((got1, got2, got3)):
            for i in range(8):
                gs[k, 2 * i : 2 * i + 2, :] = got[:, d + 128 * i : d + 128 * i + 128]
            parts.append(gs[k])
        factors, (ms, mt, ls, lt, cross, valid) = unite(parts)
        lse_s = ms + jnp.log(ls)
        lse_t = mt + jnp.log(lt)
        gain = valid * (objective_scale * smoothing_divisor)
        grad = gain * (jnp.exp(student[...] - lse_s) - jnp.exp(scaled[...] - lse_t))
        for b in range(4):
            j = row_of(b, x, c)
            for k in range(4):
                gr[pl.ds(4 * k + j, 1), :] = grad[4 * b + k : 4 * b + k + 1, :]
        g = gr[...].astype(jnp.bfloat16)
        copies = []

        def emit(source, target):
            copy = pltpu.make_async_copy(source, target, sems.at[len(copies)])
            copy.start()
            copies.append(copy)

        def weight_chunk(i):
            at = pl.ds(i * chunk, chunk)
            out[:, at] = lax.dot_general(
                g, hb[:, at], (((0,), (0,)), ((), ())), preferred_element_type=jnp.float32
            ).astype(jnp.bfloat16)
            emit(out.at[:, at], weight_grad.at[:, at])

        n = d // chunk
        for i in range(n // 2):
            weight_chunk(i)
        row = lax.broadcasted_iota(jnp.int32, (ROWS, 1), 0)
        home = 4 * (z ^ (row & 3)) + 2 * (x ^ ((row >> 2) & 1)) + (c ^ (row >> 3))
        value = valid * (cross / lt - lse_t + lse_s)
        lane = lax.broadcasted_iota(jnp.int32, (ROWS, STATS), 1)
        div[...] = jnp.sum(jnp.where(lane == home, value, 0.0), axis=0)[0:ROWS]
        emit(div, divergence)
        a_s = part[0:1, :] * factors[0][0:1, 0:1]
        a_t = part[1:2, :] * factors[0][0:1, 1:2]
        for got, f in zip((got1, got2, got3), factors[1:]):
            a_s = a_s + got[0:1, 0:d] * f[0:1, 0:1]
            a_t = a_t + got[1:2, 0:d] * f[0:1, 1:2]
        hid[...] = (gain[0:1] * (a_s / ls[0:1] - a_t / lt[0:1])).astype(jnp.bfloat16)
        emit(hid, hidden_grad)
        for i in range(n // 2, n):
            weight_chunk(i)
        for copy in copies:
            copy.wait()

    return last_kernel


VMEM = pl.BlockSpec(memory_space=pltpu.VMEM)
ANY = pl.BlockSpec(memory_space=pltpu.HBM)
PARAMS = pltpu.CompilerParams(vmem_limit_bytes=32 << 20)


def call(kernel, out, scratch=(), in_specs=None, out_specs=None, cost=None):
    shapes = [jax.ShapeDtypeStruct(s, t) for s, t in out]
    return lambda *a: pl.pallas_call(
        kernel,
        out_shape=shapes,
        in_specs=in_specs or [VMEM] * len(a),
        out_specs=out_specs or [VMEM] * len(out),
        scratch_shapes=list(scratch),
        compiler_params=PARAMS,
        cost_estimate=cost,
    )(*a)


def small_body(hidden_rows, mentor, head_weight, row_mask):
    f32, bf16 = jnp.float32, jnp.bfloat16
    v, d = head_weight.shape
    pieces = [lax.ppermute(hidden_rows, "vocab", flip(4, k)) for k in (1, 2, 3)]
    scaled, et, teacher, own = call(
        teacher_kernel,
        [((ROWS, v), f32), ((ROWS, v), f32), ((ROWS, STATS), f32), ((4, d), bf16)],
        [
            pltpu.VMEM((ROWS, v), f32),
            pltpu.SMEM((ROWS,), jnp.int32),
            pltpu.VMEM((ROWS // 2, 2 * v), f32),
            pltpu.SemaphoreType.DMA((3,)),
        ],
        [ANY, ANY, VMEM, ANY],
        cost=pl.CostEstimate(flops=2_000_000_000, transcendentals=ROWS * v, bytes_accessed=2 << 20),
    )(
        pltpu.with_memory_space_constraint(row_mask, pltpu.HBM),
        pltpu.with_memory_space_constraint(mentor, pltpu.HBM),
        lax.ppermute(mentor, "teach", flip(2, 1)),
        pltpu.with_memory_space_constraint(hidden_rows, pltpu.HBM),
    )
    student, stats, hb, keep, send = call(
        first_kernel,
        [((ROWS, v), f32), ((ROWS, STATS), f32), ((ROWS, d), bf16), ((16, d), f32), ((16, d + STATS), f32)],
        [
            pltpu.VMEM((ROWS, d), f32),
            pltpu.VMEM((ROWS, v), f32),
            pltpu.VMEM((2 * ROWS, v), f32),
        ],
    )(own, *pieces, head_weight, scaled, et, teacher)
    got = lax.ppermute(send, "teach", flip(2, 1))
    stats, keep, send = call(
        second_kernel, [((ROWS, STATS), f32), ((8, d), f32), ((8, d + 2 * STATS), f32)]
    )(keep, stats, got)
    got = lax.ppermute(send, "rows", flip(2, 1))
    stats, keep, *sends = call(
        third_kernel,
        [((ROWS, STATS), f32), ((2, d), f32)] + [((2, d + 8 * STATS), f32)] * 3,
        [pltpu.VMEM((ROWS, STATS), f32)],
    )(keep, stats, got)
    gots = [lax.ppermute(a, "vocab", flip(4, k)) for k, a in enumerate(sends, 1)]
    chunk = 512
    return tuple(
        call(
            make_last_kernel(chunk),
            [((ROWS,), f32), ((1, d), bf16), ((v, d), bf16)],
            [
                pltpu.VMEM((3, ROWS, STATS), f32),
                pltpu.VMEM((ROWS, v), f32),
                pltpu.VMEM((v, d), bf16),
                pltpu.VMEM((ROWS,), f32),
                pltpu.VMEM((1, d), bf16),
                pltpu.SemaphoreType.DMA((d // chunk + 2,)),
            ],
            [VMEM] * 8,
            [ANY] * 3,
        )(keep, stats, *gots, student, scaled, hb)
    )


def solution(mesh):
    sizes = mesh.shape["vocab"], mesh.shape["rows"], mesh.shape["teach"]
    general = make_body(*sizes)

    def body(hidden_rows, mentor, head_weight, row_mask):
        small = sizes == (4, 2, 2) and row_mask.shape[0] == ROWS and head_weight.shape[1] % 512 == 0
        return (small_body if small else general)(hidden_rows, mentor, head_weight, row_mask)
    return jax.shard_map(
        body,
        mesh=mesh,
        in_specs=(
            P(("groups", "vocab"), None),
            P(("groups", "teach"), ("vocab", "rows")),
            P(("vocab", "rows", "teach"), None),
            P("groups"),
        ),
        out_specs=(
            P("groups"),
            P(("groups", "vocab", "rows", "teach"), None),
            P(("groups", "vocab", "rows", "teach"), None),
        ),
        check_vma=False,
    )
```

```python
import jax
import jax.numpy as jnp
from jax import lax
from jax.experimental import pallas as pl
from jax.experimental.pallas import tpu as pltpu
from jax.sharding import PartitionSpec as P

smoothing_divisor = 2.0
objective_scale = 256.0


def flip(n, d):
    return [(i, i ^ d) for i in range(n)]


def bits(n):
    out = []
    d = 1
    while d < n:
        out.append(d)
        d *= 2
    return out


def swap(a, d):
    n = a.shape[0]
    b = a.reshape((n // (2 * d), 2, d) + a.shape[1:])
    return jnp.concatenate([b[:, 1:], b[:, :1]], axis=1).reshape(a.shape)


def relative(a, position, n, stride):
    for d in bits(n):
        a = jnp.where((position & d) != 0, swap(a, d * stride), a)
    return a


def make_body(nz, nx, nc):
    def body(hidden_rows, mentor, head_weight, row_mask):
        z, x, c = lax.axis_index("vocab"), lax.axis_index("rows"), lax.axis_index("teach")
        total = row_mask.shape[0]
        q = total // (nz * nx * nc)
        own = relative(relative(hidden_rows, c, nc, q), x, nx, q * nc)
        gathered = own
        if nz == 4:
            gathered = jnp.concatenate(
                [own] + [lax.ppermute(own, "vocab", flip(nz, k)) for k in (1, 2, 3)], 0
            )
        else:
            for d in bits(nz):
                gathered = jnp.concatenate([gathered, lax.ppermute(gathered, "vocab", flip(nz, d))], 0)
        width = mentor.shape[1] // 2
        left, right = mentor[:, :width], mentor[:, width:]
        kept = jnp.where(c == 0, left, right)
        got = lax.ppermute(jnp.where(c == 0, right, left), "teach", flip(nc, 1))
        scaled = jnp.concatenate([jnp.where(c == 0, kept, got), jnp.where(c == 0, got, kept)], 0)

        def rel(a):
            a = relative(a, c, nc, q)
            a = relative(a, x, nx, q * nc)
            return relative(a, z, nz, q * nc * nx)

        scaled = rel(scaled) / smoothing_divisor
        mask = rel(row_mask).astype(jnp.float32)
        student = (
            lax.dot_general(
                gathered, head_weight, (((1,), (1,)), ((), ())), preferred_element_type=jnp.float32
            )
            / smoothing_divisor
        )
        ms = jnp.max(student, axis=1)
        mt = jnp.max(scaled, axis=1)
        es = jnp.exp(student - ms[:, None])
        et = jnp.exp(scaled - mt[:, None])
        stats = jnp.stack(
            [ms, mt, jnp.sum(es, axis=1), jnp.sum(et, axis=1), jnp.sum(et * (scaled - student), axis=1)], 0
        )
        both = jnp.concatenate([es, et], 0)
        high = both.astype(jnp.bfloat16)
        low = (both - high.astype(jnp.float32)).astype(jnp.bfloat16)
        part = jnp.dot(
            jnp.concatenate([high, low], 0), head_weight, preferred_element_type=jnp.float32
        )
        part = part[: 2 * total] + part[2 * total :]
        part = part.reshape(2, nz, nx, nc, q, -1)

        def merge(keep, stats, others):
            top = stats[:2]
            for _, s in others:
                top = jnp.maximum(top, s[:2])
            factor = [jnp.exp(s[:2] - top) for s in [stats] + [s for _, s in others]]
            sums = sum(
                jnp.concatenate([f * s[2:4], (f[1] * s[4])[None]], 0)
                for f, s in zip(factor, [stats] + [s for _, s in others])
            )
            return top, factor, jnp.concatenate([top, sums], 0)

        def level(part, stats, axis, n, dim, stride):
            if n == 4:
                steps = [(1, 2, 3)]
            else:
                steps = [(d,) for d in reversed(bits(n))]
            size = n
            for ds in steps:
                span = size // (len(ds) + 1)
                keep = lax.slice_in_dim(part, 0, span, axis=dim)
                others = []
                for d in ds:
                    a = lax.ppermute(lax.slice_in_dim(part, d, d + span, axis=dim), axis, flip(n, d))
                    s = lax.ppermute(stats, axis, flip(n, d))
                    s = s.T
                    for b in bits(n):
                        if d & b:
                            s = swap(s, b * stride)
                    others.append((a, s.T))
                _, factor, stats = merge(keep, stats, others)
                rows = [f.reshape(2, nz, nx, nc, q, 1) for f in factor]

                def cut(f):
                    shape = keep.shape
                    for ax in range(1, 4):
                        f = lax.slice_in_dim(f, 0, shape[ax], axis=ax)
                    return f

                part = keep * cut(rows[0])
                for (a, _), f in zip(others, rows[1:]):
                    part = part + a * cut(f)
                size = span
            return part, stats

        part, stats = level(part, stats, "teach", nc, 3, q)
        part, stats = level(part, stats, "rows", nx, 2, q * nc)
        part, stats = level(part, stats, "vocab", nz, 1, q * nc * nx)
        part = part.reshape(2, q, -1)
        ms, mt, ls, lt, cross = stats
        lse_s = ms + jnp.log(ls)
        lse_t = mt + jnp.log(lt)
        divergence = rel(mask * (cross / lt - lse_t + lse_s))
        gain = mask * (objective_scale * smoothing_divisor)
        grad = (
            gain[:, None] * (jnp.exp(student - lse_s[:, None]) - jnp.exp(scaled - lse_t[:, None]))
        ).astype(jnp.bfloat16)
        weight_grad = lax.dot_general(
            grad, gathered, (((0,), (0,)), ((), ())), preferred_element_type=jnp.float32
        )
        hidden_grad = gain[:q, None] * (part[0] / ls[:q, None] - part[1] / lt[:q, None])
        return divergence, hidden_grad.astype(jnp.bfloat16), weight_grad.astype(jnp.bfloat16)

    return body


ROWS = 16
STATS = 128


def pack(columns):
    lane = lax.broadcasted_iota(jnp.int32, (ROWS, STATS), 1)
    out = jnp.zeros((ROWS, STATS), jnp.float32)
    for i, column in enumerate(columns):
        out = jnp.where(lane == i, column, out)
    return out


def unite(parts):
    top = parts[0]
    for s in parts[1:]:
        top = jnp.maximum(top, s)
    factors = [jnp.exp(s - top) for s in parts]
    ls = sum(s[:, 2:3] * f[:, 0:1] for s, f in zip(parts, factors))
    lt = sum(s[:, 3:4] * f[:, 1:2] for s, f in zip(parts, factors))
    cross = sum(s[:, 4:5] * f[:, 1:2] for s, f in zip(parts, factors))
    return factors, [top[:, 0:1], top[:, 1:2], ls, lt, cross, top[:, 5:6]]


def places():
    return lax.axis_index("vocab"), lax.axis_index("rows"), lax.axis_index("teach")


def row_of(b, x, c):
    return 2 * (x ^ (b & 1)) + (c ^ (b >> 1))


def entry_kernel(mask_in, own_in, h_in, valid_out, own, h, mask, sems):
    pairs = ((mask_in, mask), (h_in, h), (own_in, own))
    copies = [pltpu.make_async_copy(a, b, sems.at[i]) for i, (a, b) in enumerate(pairs)]
    for copy in copies:
        copy.start()
    z, x, c = places()
    copies[0].wait()
    row = lax.broadcasted_iota(jnp.int32, (ROWS, STATS), 0)
    valid = jnp.zeros((ROWS, STATS), jnp.float32)
    for r in range(ROWS):
        at = 4 * ((r & 3) ^ z) + row_of(r >> 2, x, c)
        valid = jnp.where(row == r, mask[at].astype(jnp.float32), valid)
    valid_out[...] = valid
    copies[1].wait()
    copies[2].wait()


def teacher_kernel(valid, own, got, scaled, et, stats, tt):
    z, x, c = places()
    v = scaled.shape[1]
    for i, tile in ((c, own[...]), (1 - c, got[...])):
        tt[pl.ds(pl.multiple_of(8 * i, 8), 8), :] = 0.5 * jnp.where(c == 0, tile[:, 0:v], tile[:, v : 2 * v])
    for r in range(ROWS):
        scaled[r : r + 1, :] = tt[pl.ds(4 * ((r & 3) ^ z) + row_of(r >> 2, x, c), 1), :]
    t = scaled[...]
    mt = jnp.max(t, axis=1, keepdims=True)
    e = jnp.exp(t - mt)
    et[...] = e
    none = jnp.zeros_like(mt)
    stats[...] = pack([none, mt, none, jnp.sum(e, axis=1, keepdims=True), none, valid[:, 5:6]])


def first_kernel(h0, h1, h2, h3, w, scaled, et_in, teacher, student, stats, hb, keep, send, hf, raw, e):
    z, x, c = places()
    for k, h in enumerate((h0, h1, h2, h3)):
        hf[4 * k : 4 * k + 4, :] = h[...].astype(jnp.float32)
    rows = hf[...].astype(jnp.bfloat16)
    hb[...] = rows
    raw[...] = 0.5 * lax.dot_general(
        rows, w[...], (((1,), (1,)), ((), ())), preferred_element_type=jnp.float32
    )

    @pl.when(z >= 0)
    def _():
        for b in range(4):
            j = row_of(b, x, c)
            for k in range(4):
                student[4 * b + k : 4 * b + k + 1, :] = raw[pl.ds(4 * k + j, 1), :]
        s = student[...]
        t = scaled[...]
        et = et_in[...]
        ms = jnp.max(s, axis=1, keepdims=True)
        es = jnp.exp(s - ms)
        st = pack(
            [
                ms,
                teacher[:, 1:2],
                jnp.sum(es, axis=1, keepdims=True),
                teacher[:, 3:4],
                jnp.sum(et * (t - s), axis=1, keepdims=True),
                teacher[:, 5:6],
            ]
        )
        stats[...] = st
        for b in range(4):
            e[8 * b : 8 * b + 4, :] = es[4 * b : 4 * b + 4, :]
            e[8 * b + 4 : 8 * b + 8, :] = et[4 * b : 4 * b + 4, :]
        both = e[...]
        high = both.astype(jnp.bfloat16)
        low = (both - high.astype(jnp.float32)).astype(jnp.bfloat16)
        part = jnp.dot(jnp.concatenate([high, low], 0), w[...], preferred_element_type=jnp.float32)
        d = part.shape[1]
        keep[...] = part[0:16] + part[32:48]
        send[:, 0:d] = part[16:32] + part[48:64]
        send[0:8, d:] = st[8:16]
        send[8:16, d:] = st[0:8]


def second_kernel(part, stats, got, stats_out, keep, send):
    d = part.shape[1]
    factors, columns = unite([stats[...], got[:, d:]])
    st = pack(columns)
    stats_out[...] = st
    scale = [
        jnp.concatenate([f[0:4, 0:1], f[0:4, 1:2], f[4:8, 0:1], f[4:8, 1:2]], 0) for f in factors
    ]
    total = part[...] * scale[0] + got[:, 0:d] * scale[1]
    keep[...] = total[0:8]
    send[:, 0:d] = total[8:16]
    for i in range(2):
        send[0:4, d + 128 * i : d + 128 * i + 128] = st[8 * i + 4 : 8 * i + 8]
        send[4:8, d + 128 * i : d + 128 * i + 128] = st[8 * i : 8 * i + 4]


def third_kernel(part, stats, got, stats_out, keep, send1, send2, send3, gs):
    d = part.shape[1]
    for i in range(2):
        gs[8 * i : 8 * i + 8, :] = got[:, d + 128 * i : d + 128 * i + 128]
    factors, columns = unite([stats[...], gs[...]])
    st = pack(columns)
    stats_out[...] = st
    scale = [jnp.concatenate([f[0:4, 0:1], f[0:4, 1:2]], 0) for f in factors]
    total = part[...] * scale[0] + got[:, 0:d] * scale[1]
    keep[0:1, :] = total[0:1]
    keep[1:2, :] = total[4:5]
    for k, send in enumerate((send1, send2, send3), 1):
        send[0:1, 0:d] = total[k : k + 1]
        send[1:2, 0:d] = total[4 + k : 5 + k]
        for p in range(ROWS):
            at = d + 128 * (p // 2)
            r = p ^ k
            send[p % 2 : p % 2 + 1, at : at + 128] = st[r : r + 1]


def make_last_kernel(chunk):
    def last_kernel(
        part, stats, got1, got2, got3, student, scaled, hb,
        divergence, hidden_grad, weight_grad, gs, gr, out, div, hid, sems,
    ):
        z, x, c = places()
        d = part.shape[1]
        parts = [stats[...]]
        for k, got in enumerate((got1, got2, got3)):
            for i in range(8):
                gs[k, 2 * i : 2 * i + 2, :] = got[:, d + 128 * i : d + 128 * i + 128]
            parts.append(gs[k])
        factors, (ms, mt, ls, lt, cross, valid) = unite(parts)
        lse_s = ms + jnp.log(ls)
        lse_t = mt + jnp.log(lt)
        gain = valid * (objective_scale * smoothing_divisor)
        grad = gain * (jnp.exp(student[...] - lse_s) - jnp.exp(scaled[...] - lse_t))
        for b in range(4):
            j = row_of(b, x, c)
            for k in range(4):
                gr[pl.ds(4 * k + j, 1), :] = grad[4 * b + k : 4 * b + k + 1, :]
        g = gr[...].astype(jnp.bfloat16)
        copies = []

        def emit(source, target):
            copy = pltpu.make_async_copy(source, target, sems.at[len(copies)])
            copy.start()
            copies.append(copy)

        def weight_chunk(i):
            at = pl.ds(i * chunk, chunk)
            out[:, at] = lax.dot_general(
                g, hb[:, at], (((0,), (0,)), ((), ())), preferred_element_type=jnp.float32
            ).astype(jnp.bfloat16)
            emit(out.at[:, at], weight_grad.at[:, at])

        n = d // chunk
        for i in range(n // 2):
            weight_chunk(i)
        row = lax.broadcasted_iota(jnp.int32, (ROWS, 1), 0)
        home = 4 * (z ^ (row & 3)) + 2 * (x ^ ((row >> 2) & 1)) + (c ^ (row >> 3))
        value = valid * (cross / lt - lse_t + lse_s)
        lane = lax.broadcasted_iota(jnp.int32, (ROWS, STATS), 1)
        div[...] = jnp.sum(jnp.where(lane == home, value, 0.0), axis=0)[0:ROWS]
        emit(div, divergence)
        a_s = part[0:1, :] * factors[0][0:1, 0:1]
        a_t = part[1:2, :] * factors[0][0:1, 1:2]
        for got, f in zip((got1, got2, got3), factors[1:]):
            a_s = a_s + got[0:1, 0:d] * f[0:1, 0:1]
            a_t = a_t + got[1:2, 0:d] * f[0:1, 1:2]
        hid[...] = (gain[0:1] * (a_s / ls[0:1] - a_t / lt[0:1])).astype(jnp.bfloat16)
        emit(hid, hidden_grad)
        for i in range(n // 2, n):
            weight_chunk(i)
        for copy in copies:
            copy.wait()

    return last_kernel


VMEM = pl.BlockSpec(memory_space=pltpu.VMEM)
ANY = pl.BlockSpec(memory_space=pltpu.HBM)
PARAMS = pltpu.CompilerParams(vmem_limit_bytes=32 << 20)


def call(kernel, out, scratch=(), in_specs=None, out_specs=None, cost=None):
    shapes = [jax.ShapeDtypeStruct(s, t) for s, t in out]
    return lambda *a: pl.pallas_call(
        kernel,
        out_shape=shapes,
        in_specs=in_specs or [VMEM] * len(a),
        out_specs=out_specs or [VMEM] * len(out),
        scratch_shapes=list(scratch),
        compiler_params=PARAMS,
        cost_estimate=cost,
    )(*a)


def small_body(hidden_rows, mentor, head_weight, row_mask):
    f32, bf16 = jnp.float32, jnp.bfloat16
    v, d = head_weight.shape
    valid, tile, own = call(
        entry_kernel,
        [((ROWS, STATS), f32), (mentor.shape, f32), ((4, d), bf16)],
        [pltpu.SMEM((ROWS,), jnp.int32), pltpu.SemaphoreType.DMA((3,))],
        [ANY] * 3,
    )(*(pltpu.with_memory_space_constraint(a, pltpu.HBM) for a in (row_mask, mentor, hidden_rows)))
    pieces = [lax.ppermute(own, "vocab", flip(4, k)) for k in (1, 2, 3)]
    scaled, et, teacher = call(
        teacher_kernel,
        [((ROWS, v), f32), ((ROWS, v), f32), ((ROWS, STATS), f32)],
        [pltpu.VMEM((ROWS, v), f32)],
        cost=pl.CostEstimate(flops=2_000_000_000, transcendentals=ROWS * v, bytes_accessed=2 << 20),
    )(valid, tile, lax.ppermute(tile, "teach", flip(2, 1)))
    student, stats, hb, keep, send = call(
        first_kernel,
        [((ROWS, v), f32), ((ROWS, STATS), f32), ((ROWS, d), bf16), ((16, d), f32), ((16, d + STATS), f32)],
        [
            pltpu.VMEM((ROWS, d), f32),
            pltpu.VMEM((ROWS, v), f32),
            pltpu.VMEM((2 * ROWS, v), f32),
        ],
    )(own, *pieces, head_weight, scaled, et, teacher)
    got = lax.ppermute(send, "teach", flip(2, 1))
    stats, keep, send = call(
        second_kernel, [((ROWS, STATS), f32), ((8, d), f32), ((8, d + 2 * STATS), f32)]
    )(keep, stats, got)
    got = lax.ppermute(send, "rows", flip(2, 1))
    stats, keep, *sends = call(
        third_kernel,
        [((ROWS, STATS), f32), ((2, d), f32)] + [((2, d + 8 * STATS), f32)] * 3,
        [pltpu.VMEM((ROWS, STATS), f32)],
    )(keep, stats, got)
    gots = [lax.ppermute(a, "vocab", flip(4, k)) for k, a in enumerate(sends, 1)]
    chunk = 512
    return tuple(
        call(
            make_last_kernel(chunk),
            [((ROWS,), f32), ((1, d), bf16), ((v, d), bf16)],
            [
                pltpu.VMEM((3, ROWS, STATS), f32),
                pltpu.VMEM((ROWS, v), f32),
                pltpu.VMEM((v, d), bf16),
                pltpu.VMEM((ROWS,), f32),
                pltpu.VMEM((1, d), bf16),
                pltpu.SemaphoreType.DMA((d // chunk + 2,)),
            ],
            [VMEM] * 8,
            [ANY] * 3,
        )(keep, stats, *gots, student, scaled, hb)
    )


def solution(mesh):
    sizes = mesh.shape["vocab"], mesh.shape["rows"], mesh.shape["teach"]
    general = make_body(*sizes)

    def body(hidden_rows, mentor, head_weight, row_mask):
        small = sizes == (4, 2, 2) and row_mask.shape[0] == ROWS and head_weight.shape[1] % 512 == 0
        return (small_body if small else general)(hidden_rows, mentor, head_weight, row_mask)
    return jax.shard_map(
        body,
        mesh=mesh,
        in_specs=(
            P(("groups", "vocab"), None),
            P(("groups", "teach"), ("vocab", "rows")),
            P(("vocab", "rows", "teach"), None),
            P("groups"),
        ),
        out_specs=(
            P("groups"),
            P(("groups", "vocab", "rows", "teach"), None),
            P(("groups", "vocab", "rows", "teach"), None),
        ),
        check_vma=False,
    )
```

```python
import jax
import jax.numpy as jnp
from jax import lax
from jax.experimental import pallas as pl
from jax.experimental.pallas import tpu as pltpu
from jax.sharding import PartitionSpec as P

smoothing_divisor = 2.0
objective_scale = 256.0


def flip(n, d):
    return [(i, i ^ d) for i in range(n)]


def bits(n):
    out = []
    d = 1
    while d < n:
        out.append(d)
        d *= 2
    return out


def swap(a, d):
    n = a.shape[0]
    b = a.reshape((n // (2 * d), 2, d) + a.shape[1:])
    return jnp.concatenate([b[:, 1:], b[:, :1]], axis=1).reshape(a.shape)


def relative(a, position, n, stride):
    for d in bits(n):
        a = jnp.where((position & d) != 0, swap(a, d * stride), a)
    return a


def make_body(nz, nx, nc):
    def body(hidden_rows, mentor, head_weight, row_mask):
        z, x, c = lax.axis_index("vocab"), lax.axis_index("rows"), lax.axis_index("teach")
        total = row_mask.shape[0]
        q = total // (nz * nx * nc)
        own = relative(relative(hidden_rows, c, nc, q), x, nx, q * nc)
        gathered = own
        if nz == 4:
            gathered = jnp.concatenate(
                [own] + [lax.ppermute(own, "vocab", flip(nz, k)) for k in (1, 2, 3)], 0
            )
        else:
            for d in bits(nz):
                gathered = jnp.concatenate([gathered, lax.ppermute(gathered, "vocab", flip(nz, d))], 0)
        width = mentor.shape[1] // 2
        left, right = mentor[:, :width], mentor[:, width:]
        kept = jnp.where(c == 0, left, right)
        got = lax.ppermute(jnp.where(c == 0, right, left), "teach", flip(nc, 1))
        scaled = jnp.concatenate([jnp.where(c == 0, kept, got), jnp.where(c == 0, got, kept)], 0)

        def rel(a):
            a = relative(a, c, nc, q)
            a = relative(a, x, nx, q * nc)
            return relative(a, z, nz, q * nc * nx)

        scaled = rel(scaled) / smoothing_divisor
        mask = rel(row_mask).astype(jnp.float32)
        student = (
            lax.dot_general(
                gathered, head_weight, (((1,), (1,)), ((), ())), preferred_element_type=jnp.float32
            )
            / smoothing_divisor
        )
        ms = jnp.max(student, axis=1)
        mt = jnp.max(scaled, axis=1)
        es = jnp.exp(student - ms[:, None])
        et = jnp.exp(scaled - mt[:, None])
        stats = jnp.stack(
            [ms, mt, jnp.sum(es, axis=1), jnp.sum(et, axis=1), jnp.sum(et * (scaled - student), axis=1)], 0
        )
        both = jnp.concatenate([es, et], 0)
        high = both.astype(jnp.bfloat16)
        low = (both - high.astype(jnp.float32)).astype(jnp.bfloat16)
        part = jnp.dot(
            jnp.concatenate([high, low], 0), head_weight, preferred_element_type=jnp.float32
        )
        part = part[: 2 * total] + part[2 * total :]
        part = part.reshape(2, nz, nx, nc, q, -1)

        def merge(keep, stats, others):
            top = stats[:2]
            for _, s in others:
                top = jnp.maximum(top, s[:2])
            factor = [jnp.exp(s[:2] - top) for s in [stats] + [s for _, s in others]]
            sums = sum(
                jnp.concatenate([f * s[2:4], (f[1] * s[4])[None]], 0)
                for f, s in zip(factor, [stats] + [s for _, s in others])
            )
            return top, factor, jnp.concatenate([top, sums], 0)

        def level(part, stats, axis, n, dim, stride):
            if n == 4:
                steps = [(1, 2, 3)]
            else:
                steps = [(d,) for d in reversed(bits(n))]
            size = n
            for ds in steps:
                span = size // (len(ds) + 1)
                keep = lax.slice_in_dim(part, 0, span, axis=dim)
                others = []
                for d in ds:
                    a = lax.ppermute(lax.slice_in_dim(part, d, d + span, axis=dim), axis, flip(n, d))
                    s = lax.ppermute(stats, axis, flip(n, d))
                    s = s.T
                    for b in bits(n):
                        if d & b:
                            s = swap(s, b * stride)
                    others.append((a, s.T))
                _, factor, stats = merge(keep, stats, others)
                rows = [f.reshape(2, nz, nx, nc, q, 1) for f in factor]

                def cut(f):
                    shape = keep.shape
                    for ax in range(1, 4):
                        f = lax.slice_in_dim(f, 0, shape[ax], axis=ax)
                    return f

                part = keep * cut(rows[0])
                for (a, _), f in zip(others, rows[1:]):
                    part = part + a * cut(f)
                size = span
            return part, stats

        part, stats = level(part, stats, "teach", nc, 3, q)
        part, stats = level(part, stats, "rows", nx, 2, q * nc)
        part, stats = level(part, stats, "vocab", nz, 1, q * nc * nx)
        part = part.reshape(2, q, -1)
        ms, mt, ls, lt, cross = stats
        lse_s = ms + jnp.log(ls)
        lse_t = mt + jnp.log(lt)
        divergence = rel(mask * (cross / lt - lse_t + lse_s))
        gain = mask * (objective_scale * smoothing_divisor)
        grad = (
            gain[:, None] * (jnp.exp(student - lse_s[:, None]) - jnp.exp(scaled - lse_t[:, None]))
        ).astype(jnp.bfloat16)
        weight_grad = lax.dot_general(
            grad, gathered, (((0,), (0,)), ((), ())), preferred_element_type=jnp.float32
        )
        hidden_grad = gain[:q, None] * (part[0] / ls[:q, None] - part[1] / lt[:q, None])
        return divergence, hidden_grad.astype(jnp.bfloat16), weight_grad.astype(jnp.bfloat16)

    return body


ROWS = 16
STATS = 128


def pack(columns):
    lane = lax.broadcasted_iota(jnp.int32, (ROWS, STATS), 1)
    out = jnp.zeros((ROWS, STATS), jnp.float32)
    for i, column in enumerate(columns):
        out = jnp.where(lane == i, column, out)
    return out


def unite(parts):
    top = parts[0]
    for s in parts[1:]:
        top = jnp.maximum(top, s)
    factors = [jnp.exp(s - top) for s in parts]
    ls = sum(s[:, 2:3] * f[:, 0:1] for s, f in zip(parts, factors))
    lt = sum(s[:, 3:4] * f[:, 1:2] for s, f in zip(parts, factors))
    cross = sum(s[:, 4:5] * f[:, 1:2] for s, f in zip(parts, factors))
    return factors, [top[:, 0:1], top[:, 1:2], ls, lt, cross, top[:, 5:6]]


def places():
    return lax.axis_index("vocab"), lax.axis_index("rows"), lax.axis_index("teach")


def row_of(b, x, c):
    return 2 * (x ^ (b & 1)) + (c ^ (b >> 1))


def entry_kernel(mask_in, own_in, h_in, valid_out, own, h, mask, sems):
    pairs = ((mask_in, mask), (h_in, h), (own_in, own))
    copies = [pltpu.make_async_copy(a, b, sems.at[i]) for i, (a, b) in enumerate(pairs)]
    for copy in copies:
        copy.start()
    z, x, c = places()
    copies[0].wait()
    row = lax.broadcasted_iota(jnp.int32, (ROWS, STATS), 0)
    valid = jnp.zeros((ROWS, STATS), jnp.float32)
    for r in range(ROWS):
        at = 4 * ((r & 3) ^ z) + row_of(r >> 2, x, c)
        valid = jnp.where(row == r, mask[at].astype(jnp.float32), valid)
    valid_out[...] = valid
    copies[1].wait()
    copies[2].wait()


def teacher_kernel(valid, own, got, scaled, et, stats, tt):
    z, x, c = places()
    v = scaled.shape[1]
    for i, tile in ((c, own[...]), (1 - c, got[...])):
        tt[pl.ds(pl.multiple_of(8 * i, 8), 8), :] = 0.5 * jnp.where(c == 0, tile[:, 0:v], tile[:, v : 2 * v])
    for r in range(ROWS):
        scaled[r : r + 1, :] = tt[pl.ds(4 * ((r & 3) ^ z) + row_of(r >> 2, x, c), 1), :]
    t = scaled[...]
    mt = jnp.max(t, axis=1, keepdims=True)
    e = jnp.exp(t - mt)
    et[...] = e
    none = jnp.zeros_like(mt)
    stats[...] = pack([none, mt, none, jnp.sum(e, axis=1, keepdims=True), none, valid[:, 5:6]])


def first_kernel(h0, h1, h2, h3, w, scaled, et_in, teacher, student, stats, hb, keep, send, hf, raw, e):
    z, x, c = places()
    for k, h in enumerate((h0, h1, h2, h3)):
        hf[4 * k : 4 * k + 4, :] = h[...].astype(jnp.float32)
    rows = hf[...].astype(jnp.bfloat16)
    hb[...] = rows
    raw[...] = 0.5 * lax.dot_general(
        rows, w[...], (((1,), (1,)), ((), ())), preferred_element_type=jnp.float32
    )

    @pl.when(z >= 0)
    def _():
        for b in range(4):
            j = row_of(b, x, c)
            for k in range(4):
                student[4 * b + k : 4 * b + k + 1, :] = raw[pl.ds(4 * k + j, 1), :]
        s = student[...]
        t = scaled[...]
        et = et_in[...]
        ms = jnp.max(s, axis=1, keepdims=True)
        es = jnp.exp(s - ms)
        st = pack(
            [
                ms,
                teacher[:, 1:2],
                jnp.sum(es, axis=1, keepdims=True),
                teacher[:, 3:4],
                jnp.sum(et * (t - s), axis=1, keepdims=True),
                teacher[:, 5:6],
            ]
        )
        stats[...] = st
        for b in range(4):
            e[8 * b : 8 * b + 4, :] = es[4 * b : 4 * b + 4, :]
            e[8 * b + 4 : 8 * b + 8, :] = et[4 * b : 4 * b + 4, :]
        both = e[...]
        high = both.astype(jnp.bfloat16)
        low = (both - high.astype(jnp.float32)).astype(jnp.bfloat16)
        part = jnp.dot(jnp.concatenate([high, low], 0), w[...], preferred_element_type=jnp.float32)
        d = part.shape[1]
        keep[...] = part[0:16] + part[32:48]
        send[:, 0:d] = part[16:32] + part[48:64]
        send[0:8, d:] = st[8:16]
        send[8:16, d:] = st[0:8]


def second_kernel(part, stats, got, stats_out, keep, send):
    d = part.shape[1]
    factors, columns = unite([stats[...], got[:, d:]])
    st = pack(columns)
    stats_out[...] = st
    scale = [
        jnp.concatenate([f[0:4, 0:1], f[0:4, 1:2], f[4:8, 0:1], f[4:8, 1:2]], 0) for f in factors
    ]
    total = part[...] * scale[0] + got[:, 0:d] * scale[1]
    keep[...] = total[0:8]
    send[:, 0:d] = total[8:16]
    for i in range(2):
        send[0:4, d + 128 * i : d + 128 * i + 128] = st[8 * i + 4 : 8 * i + 8]
        send[4:8, d + 128 * i : d + 128 * i + 128] = st[8 * i : 8 * i + 4]


def third_kernel(part, stats, got, stats_out, keep, send3, send2, send1, gs):
    d = part.shape[1]
    for i in range(2):
        gs[8 * i : 8 * i + 8, :] = got[:, d + 128 * i : d + 128 * i + 128]
    factors, columns = unite([stats[...], gs[...]])
    st = pack(columns)
    stats_out[...] = st
    scale = [jnp.concatenate([f[0:4, 0:1], f[0:4, 1:2]], 0) for f in factors]
    total = part[...] * scale[0] + got[:, 0:d] * scale[1]
    keep[0:1, :] = total[0:1]
    keep[1:2, :] = total[4:5]
    for k, send in enumerate((send1, send2, send3), 1):
        send[0:1, 0:d] = total[k : k + 1]
        send[1:2, 0:d] = total[4 + k : 5 + k]
        for p in range(ROWS):
            at = d + 128 * (p // 2)
            r = p ^ k
            send[p % 2 : p % 2 + 1, at : at + 128] = st[r : r + 1]


def make_last_kernel(chunk):
    def last_kernel(
        part, stats, got3, got2, got1, student, scaled, hb,
        divergence, hidden_grad, weight_grad, gs, gr, out, div, hid, sems,
    ):
        z, x, c = places()
        d = part.shape[1]
        parts = [stats[...]]
        for k, got in enumerate((got1, got2, got3)):
            for i in range(8):
                gs[k, 2 * i : 2 * i + 2, :] = got[:, d + 128 * i : d + 128 * i + 128]
            parts.append(gs[k])
        factors, (ms, mt, ls, lt, cross, valid) = unite(parts)
        lse_s = ms + jnp.log(ls)
        lse_t = mt + jnp.log(lt)
        gain = valid * (objective_scale * smoothing_divisor)
        grad = gain * (jnp.exp(student[...] - lse_s) - jnp.exp(scaled[...] - lse_t))
        for b in range(4):
            j = row_of(b, x, c)
            for k in range(4):
                gr[pl.ds(4 * k + j, 1), :] = grad[4 * b + k : 4 * b + k + 1, :]
        g = gr[...].astype(jnp.bfloat16)
        copies = []

        def emit(source, target):
            copy = pltpu.make_async_copy(source, target, sems.at[len(copies)])
            copy.start()
            copies.append(copy)

        def weight_chunk(i):
            at = pl.ds(i * chunk, chunk)
            out[:, at] = lax.dot_general(
                g, hb[:, at], (((0,), (0,)), ((), ())), preferred_element_type=jnp.float32
            ).astype(jnp.bfloat16)
            emit(out.at[:, at], weight_grad.at[:, at])

        n = d // chunk
        for i in range(n // 2):
            weight_chunk(i)
        row = lax.broadcasted_iota(jnp.int32, (ROWS, 1), 0)
        home = 4 * (z ^ (row & 3)) + 2 * (x ^ ((row >> 2) & 1)) + (c ^ (row >> 3))
        value = valid * (cross / lt - lse_t + lse_s)
        lane = lax.broadcasted_iota(jnp.int32, (ROWS, STATS), 1)
        div[...] = jnp.sum(jnp.where(lane == home, value, 0.0), axis=0)[0:ROWS]
        emit(div, divergence)
        a_s = part[0:1, :] * factors[0][0:1, 0:1]
        a_t = part[1:2, :] * factors[0][0:1, 1:2]
        for got, f in zip((got1, got2, got3), factors[1:]):
            a_s = a_s + got[0:1, 0:d] * f[0:1, 0:1]
            a_t = a_t + got[1:2, 0:d] * f[0:1, 1:2]
        hid[...] = (gain[0:1] * (a_s / ls[0:1] - a_t / lt[0:1])).astype(jnp.bfloat16)
        emit(hid, hidden_grad)
        for i in range(n // 2, n):
            weight_chunk(i)
        for copy in copies:
            copy.wait()

    return last_kernel


VMEM = pl.BlockSpec(memory_space=pltpu.VMEM)
ANY = pl.BlockSpec(memory_space=pltpu.HBM)
PARAMS = pltpu.CompilerParams(vmem_limit_bytes=32 << 20)


def call(kernel, out, scratch=(), in_specs=None, out_specs=None, cost=None):
    shapes = [jax.ShapeDtypeStruct(s, t) for s, t in out]
    return lambda *a: pl.pallas_call(
        kernel,
        out_shape=shapes,
        in_specs=in_specs or [VMEM] * len(a),
        out_specs=out_specs or [VMEM] * len(out),
        scratch_shapes=list(scratch),
        compiler_params=PARAMS,
        cost_estimate=cost,
    )(*a)


def small_body(hidden_rows, mentor, head_weight, row_mask):
    f32, bf16 = jnp.float32, jnp.bfloat16
    v, d = head_weight.shape
    valid, tile, own = call(
        entry_kernel,
        [((ROWS, STATS), f32), (mentor.shape, f32), ((4, d), bf16)],
        [pltpu.SMEM((ROWS,), jnp.int32), pltpu.SemaphoreType.DMA((3,))],
        [ANY] * 3,
        cost=pl.CostEstimate(flops=2_000_000_000, transcendentals=0, bytes_accessed=2 << 20),
    )(*(pltpu.with_memory_space_constraint(a, pltpu.HBM) for a in (row_mask, mentor, hidden_rows)))
    pieces = [lax.ppermute(own, "vocab", flip(4, k)) for k in (1, 2, 3)]
    scaled, et, teacher = call(
        teacher_kernel,
        [((ROWS, v), f32), ((ROWS, v), f32), ((ROWS, STATS), f32)],
        [pltpu.VMEM((ROWS, v), f32)],
    )(valid, tile, lax.ppermute(tile, "teach", flip(2, 1)))
    student, stats, hb, keep, send = call(
        first_kernel,
        [((ROWS, v), f32), ((ROWS, STATS), f32), ((ROWS, d), bf16), ((16, d), f32), ((16, d + STATS), f32)],
        [
            pltpu.VMEM((ROWS, d), f32),
            pltpu.VMEM((ROWS, v), f32),
            pltpu.VMEM((2 * ROWS, v), f32),
        ],
    )(own, *pieces, head_weight, scaled, et, teacher)
    got = lax.ppermute(send, "teach", flip(2, 1))
    stats, keep, send = call(
        second_kernel, [((ROWS, STATS), f32), ((8, d), f32), ((8, d + 2 * STATS), f32)]
    )(keep, stats, got)
    got = lax.ppermute(send, "rows", flip(2, 1))
    stats, keep, *sends = call(
        third_kernel,
        [((ROWS, STATS), f32), ((2, d), f32)] + [((2, d + 8 * STATS), f32)] * 3,
        [pltpu.VMEM((ROWS, STATS), f32)],
    )(keep, stats, got)
    gots = [lax.ppermute(a, "vocab", flip(4, k)) for k, a in zip((3, 2, 1), sends)]
    chunk = 512
    return tuple(
        call(
            make_last_kernel(chunk),
            [((ROWS,), f32), ((1, d), bf16), ((v, d), bf16)],
            [
                pltpu.VMEM((3, ROWS, STATS), f32),
                pltpu.VMEM((ROWS, v), f32),
                pltpu.VMEM((v, d), bf16),
                pltpu.VMEM((ROWS,), f32),
                pltpu.VMEM((1, d), bf16),
                pltpu.SemaphoreType.DMA((d // chunk + 2,)),
            ],
            [VMEM] * 8,
            [ANY] * 3,
        )(keep, stats, *gots, student, scaled, hb)
    )


def solution(mesh):
    sizes = mesh.shape["vocab"], mesh.shape["rows"], mesh.shape["teach"]
    general = make_body(*sizes)

    def body(hidden_rows, mentor, head_weight, row_mask):
        small = sizes == (4, 2, 2) and row_mask.shape[0] == ROWS and head_weight.shape[1] % 512 == 0
        return (small_body if small else general)(hidden_rows, mentor, head_weight, row_mask)
    return jax.shard_map(
        body,
        mesh=mesh,
        in_specs=(
            P(("groups", "vocab"), None),
            P(("groups", "teach"), ("vocab", "rows")),
            P(("vocab", "rows", "teach"), None),
            P("groups"),
        ),
        out_specs=(
            P("groups"),
            P(("groups", "vocab", "rows", "teach"), None),
            P(("groups", "vocab", "rows", "teach"), None),
        ),
        check_vma=False,
    )
```

```python
import jax
import jax.numpy as jnp
from jax import lax
from jax.experimental import pallas as pl
from jax.experimental.pallas import tpu as pltpu
from jax.sharding import PartitionSpec as P

smoothing_divisor = 2.0
objective_scale = 256.0


def flip(n, d):
    return [(i, i ^ d) for i in range(n)]


def bits(n):
    out = []
    d = 1
    while d < n:
        out.append(d)
        d *= 2
    return out


def swap(a, d):
    n = a.shape[0]
    b = a.reshape((n // (2 * d), 2, d) + a.shape[1:])
    return jnp.concatenate([b[:, 1:], b[:, :1]], axis=1).reshape(a.shape)


def relative(a, position, n, stride):
    for d in bits(n):
        a = jnp.where((position & d) != 0, swap(a, d * stride), a)
    return a


def make_body(nz, nx, nc):
    def body(hidden_rows, mentor, head_weight, row_mask):
        z, x, c = lax.axis_index("vocab"), lax.axis_index("rows"), lax.axis_index("teach")
        total = row_mask.shape[0]
        q = total // (nz * nx * nc)
        own = relative(relative(hidden_rows, c, nc, q), x, nx, q * nc)
        gathered = own
        if nz == 4:
            gathered = jnp.concatenate(
                [own] + [lax.ppermute(own, "vocab", flip(nz, k)) for k in (1, 2, 3)], 0
            )
        else:
            for d in bits(nz):
                gathered = jnp.concatenate([gathered, lax.ppermute(gathered, "vocab", flip(nz, d))], 0)
        width = mentor.shape[1] // 2
        left, right = mentor[:, :width], mentor[:, width:]
        kept = jnp.where(c == 0, left, right)
        got = lax.ppermute(jnp.where(c == 0, right, left), "teach", flip(nc, 1))
        scaled = jnp.concatenate([jnp.where(c == 0, kept, got), jnp.where(c == 0, got, kept)], 0)

        def rel(a):
            a = relative(a, c, nc, q)
            a = relative(a, x, nx, q * nc)
            return relative(a, z, nz, q * nc * nx)

        scaled = rel(scaled) / smoothing_divisor
        mask = rel(row_mask).astype(jnp.float32)
        student = (
            lax.dot_general(
                gathered, head_weight, (((1,), (1,)), ((), ())), preferred_element_type=jnp.float32
            )
            / smoothing_divisor
        )
        ms = jnp.max(student, axis=1)
        mt = jnp.max(scaled, axis=1)
        es = jnp.exp(student - ms[:, None])
        et = jnp.exp(scaled - mt[:, None])
        stats = jnp.stack(
            [ms, mt, jnp.sum(es, axis=1), jnp.sum(et, axis=1), jnp.sum(et * (scaled - student), axis=1)], 0
        )
        both = jnp.concatenate([es, et], 0)
        high = both.astype(jnp.bfloat16)
        low = (both - high.astype(jnp.float32)).astype(jnp.bfloat16)
        part = jnp.dot(
            jnp.concatenate([high, low], 0), head_weight, preferred_element_type=jnp.float32
        )
        part = part[: 2 * total] + part[2 * total :]
        part = part.reshape(2, nz, nx, nc, q, -1)

        def merge(keep, stats, others):
            top = stats[:2]
            for _, s in others:
                top = jnp.maximum(top, s[:2])
            factor = [jnp.exp(s[:2] - top) for s in [stats] + [s for _, s in others]]
            sums = sum(
                jnp.concatenate([f * s[2:4], (f[1] * s[4])[None]], 0)
                for f, s in zip(factor, [stats] + [s for _, s in others])
            )
            return top, factor, jnp.concatenate([top, sums], 0)

        def level(part, stats, axis, n, dim, stride):
            if n == 4:
                steps = [(1, 2, 3)]
            else:
                steps = [(d,) for d in reversed(bits(n))]
            size = n
            for ds in steps:
                span = size // (len(ds) + 1)
                keep = lax.slice_in_dim(part, 0, span, axis=dim)
                others = []
                for d in ds:
                    a = lax.ppermute(lax.slice_in_dim(part, d, d + span, axis=dim), axis, flip(n, d))
                    s = lax.ppermute(stats, axis, flip(n, d))
                    s = s.T
                    for b in bits(n):
                        if d & b:
                            s = swap(s, b * stride)
                    others.append((a, s.T))
                _, factor, stats = merge(keep, stats, others)
                rows = [f.reshape(2, nz, nx, nc, q, 1) for f in factor]

                def cut(f):
                    shape = keep.shape
                    for ax in range(1, 4):
                        f = lax.slice_in_dim(f, 0, shape[ax], axis=ax)
                    return f

                part = keep * cut(rows[0])
                for (a, _), f in zip(others, rows[1:]):
                    part = part + a * cut(f)
                size = span
            return part, stats

        part, stats = level(part, stats, "teach", nc, 3, q)
        part, stats = level(part, stats, "rows", nx, 2, q * nc)
        part, stats = level(part, stats, "vocab", nz, 1, q * nc * nx)
        part = part.reshape(2, q, -1)
        ms, mt, ls, lt, cross = stats
        lse_s = ms + jnp.log(ls)
        lse_t = mt + jnp.log(lt)
        divergence = rel(mask * (cross / lt - lse_t + lse_s))
        gain = mask * (objective_scale * smoothing_divisor)
        grad = (
            gain[:, None] * (jnp.exp(student - lse_s[:, None]) - jnp.exp(scaled - lse_t[:, None]))
        ).astype(jnp.bfloat16)
        weight_grad = lax.dot_general(
            grad, gathered, (((0,), (0,)), ((), ())), preferred_element_type=jnp.float32
        )
        hidden_grad = gain[:q, None] * (part[0] / ls[:q, None] - part[1] / lt[:q, None])
        return divergence, hidden_grad.astype(jnp.bfloat16), weight_grad.astype(jnp.bfloat16)

    return body


ROWS = 16
STATS = 128


def pack(columns):
    lane = lax.broadcasted_iota(jnp.int32, (ROWS, STATS), 1)
    out = jnp.zeros((ROWS, STATS), jnp.float32)
    for i, column in enumerate(columns):
        out = jnp.where(lane == i, column, out)
    return out


def unite(parts):
    top = parts[0]
    for s in parts[1:]:
        top = jnp.maximum(top, s)
    factors = [jnp.exp(s - top) for s in parts]
    ls = sum(s[:, 2:3] * f[:, 0:1] for s, f in zip(parts, factors))
    lt = sum(s[:, 3:4] * f[:, 1:2] for s, f in zip(parts, factors))
    cross = sum(s[:, 4:5] * f[:, 1:2] for s, f in zip(parts, factors))
    return factors, [top[:, 0:1], top[:, 1:2], ls, lt, cross, top[:, 5:6]]


def places():
    return lax.axis_index("vocab"), lax.axis_index("rows"), lax.axis_index("teach")


def row_of(b, x, c):
    return 2 * (x ^ (b & 1)) + (c ^ (b >> 1))


def entry_kernel(mask_in, own_in, h_in, valid_out, own, h, mask, sems):
    pairs = ((mask_in, mask), (h_in, h), (own_in, own))
    copies = [pltpu.make_async_copy(a, b, sems.at[i]) for i, (a, b) in enumerate(pairs)]
    for copy in copies:
        copy.start()
    z, x, c = places()
    copies[0].wait()
    row = lax.broadcasted_iota(jnp.int32, (ROWS, STATS), 0)
    valid = jnp.zeros((ROWS, STATS), jnp.float32)
    for r in range(ROWS):
        at = 4 * ((r & 3) ^ z) + row_of(r >> 2, x, c)
        valid = jnp.where(row == r, mask[at].astype(jnp.float32), valid)
    valid_out[...] = valid
    copies[1].wait()
    copies[2].wait()


def teacher_kernel(valid, own, got, scaled, et, stats, tt):
    z, x, c = places()
    v = scaled.shape[1]
    for i, tile in ((c, own[...]), (1 - c, got[...])):
        tt[pl.ds(pl.multiple_of(8 * i, 8), 8), :] = 0.5 * jnp.where(c == 0, tile[:, 0:v], tile[:, v : 2 * v])
    for r in range(ROWS):
        scaled[r : r + 1, :] = tt[pl.ds(4 * ((r & 3) ^ z) + row_of(r >> 2, x, c), 1), :]
    t = scaled[...]
    mt = jnp.max(t, axis=1, keepdims=True)
    e = jnp.exp(t - mt)
    et[...] = e
    none = jnp.zeros_like(mt)
    stats[...] = pack([none, mt, none, jnp.sum(e, axis=1, keepdims=True), none, valid[:, 5:6]])


def first_kernel(h0, h1, h2, h3, w, scaled, et_in, teacher, student, stats, hb, keep, send, hf, raw, e):
    z, x, c = places()
    for k, h in enumerate((h0, h1, h2, h3)):
        hf[4 * k : 4 * k + 4, :] = h[...].astype(jnp.float32)
    rows = hf[...].astype(jnp.bfloat16)
    hb[...] = rows
    raw[...] = 0.5 * lax.dot_general(
        rows, w[...], (((1,), (1,)), ((), ())), preferred_element_type=jnp.float32
    )

    @pl.when(z >= 0)
    def _():
        for b in range(4):
            j = row_of(b, x, c)
            for k in range(4):
                student[4 * b + k : 4 * b + k + 1, :] = raw[pl.ds(4 * k + j, 1), :]
        s = student[...]
        t = scaled[...]
        et = et_in[...]
        ms = jnp.max(s, axis=1, keepdims=True)
        es = jnp.exp(s - ms)
        st = pack(
            [
                ms,
                teacher[:, 1:2],
                jnp.sum(es, axis=1, keepdims=True),
                teacher[:, 3:4],
                jnp.sum(et * (t - s), axis=1, keepdims=True),
                teacher[:, 5:6],
            ]
        )
        stats[...] = st
        for b in range(4):
            e[8 * b : 8 * b + 4, :] = es[4 * b : 4 * b + 4, :]
            e[8 * b + 4 : 8 * b + 8, :] = et[4 * b : 4 * b + 4, :]
        both = e[...]
        high = both.astype(jnp.bfloat16)
        low = (both - high.astype(jnp.float32)).astype(jnp.bfloat16)
        part = jnp.dot(jnp.concatenate([high, low], 0), w[...], preferred_element_type=jnp.float32)
        d = part.shape[1]
        keep[...] = part[0:16] + part[32:48]
        send[:, 0:d] = part[16:32] + part[48:64]
        send[0:8, d:] = st[8:16]
        send[8:16, d:] = st[0:8]


def second_kernel(part, stats, got, stats_out, keep, send3, send2, send1):
    d = part.shape[1]
    factors, columns = unite([stats[...], got[:, d:]])
    st = pack(columns)
    stats_out[...] = st
    scale = [
        jnp.concatenate([f[0:4, 0:1], f[0:4, 1:2], f[4:8, 0:1], f[4:8, 1:2]], 0) for f in factors
    ]
    total = part[...] * scale[0] + got[:, 0:d] * scale[1]
    for i in range(4):
        keep[i : i + 1, :] = total[4 * i : 4 * i + 1]
    for k, send in ((3, send3), (2, send2), (1, send1)):
        for i in range(4):
            send[i : i + 1, 0:d] = total[4 * i + k : 4 * i + k + 1]
        for p in range(ROWS):
            at = d + 128 * (p // 4)
            r = p ^ k
            send[p % 4 : p % 4 + 1, at : at + 128] = st[r : r + 1]


def third_kernel(part, stats, got3, got2, got1, stats_out, keep, send, gs):
    d = part.shape[1]
    parts = [stats[...]]
    gots = (got1, got2, got3)
    for k, got in enumerate(gots):
        for i in range(4):
            gs[k, 4 * i : 4 * i + 4, :] = got[:, d + 128 * i : d + 128 * i + 128]
        parts.append(gs[k])
    factors, columns = unite(parts)
    st = pack(columns)
    stats_out[...] = st
    scale = [
        jnp.concatenate([f[0:1, 0:1], f[0:1, 1:2], f[4:5, 0:1], f[4:5, 1:2]], 0) for f in factors
    ]
    total = part[...] * scale[0]
    for got, f in zip(gots, scale[1:]):
        total = total + got[:, 0:d] * f
    keep[...] = total[0:2]
    send[:, 0:d] = total[2:4]
    for p in range(ROWS):
        at = d + 128 * (p // 2)
        r = p ^ 4
        send[p % 2 : p % 2 + 1, at : at + 128] = st[r : r + 1]


def make_last_kernel(chunk):
    def last_kernel(
        part, stats, got, student, scaled, hb,
        divergence, hidden_grad, weight_grad, gs, gr, out, div, hid, sems,
    ):
        z, x, c = places()
        d = part.shape[1]
        for i in range(8):
            gs[2 * i : 2 * i + 2, :] = got[:, d + 128 * i : d + 128 * i + 128]
        factors, (ms, mt, ls, lt, cross, valid) = unite([stats[...], gs[...]])
        lse_s = ms + jnp.log(ls)
        lse_t = mt + jnp.log(lt)
        gain = valid * (objective_scale * smoothing_divisor)
        grad = gain * (jnp.exp(student[...] - lse_s) - jnp.exp(scaled[...] - lse_t))
        for b in range(4):
            j = row_of(b, x, c)
            for k in range(4):
                gr[pl.ds(4 * k + j, 1), :] = grad[4 * b + k : 4 * b + k + 1, :]
        g = gr[...].astype(jnp.bfloat16)
        copies = []

        def emit(source, target):
            copy = pltpu.make_async_copy(source, target, sems.at[len(copies)])
            copy.start()
            copies.append(copy)

        def weight_chunk(i):
            at = pl.ds(i * chunk, chunk)
            out[:, at] = lax.dot_general(
                g, hb[:, at], (((0,), (0,)), ((), ())), preferred_element_type=jnp.float32
            ).astype(jnp.bfloat16)
            emit(out.at[:, at], weight_grad.at[:, at])

        n = d // chunk
        for i in range(n // 2):
            weight_chunk(i)
        row = lax.broadcasted_iota(jnp.int32, (ROWS, 1), 0)
        home = 4 * (z ^ (row & 3)) + 2 * (x ^ ((row >> 2) & 1)) + (c ^ (row >> 3))
        value = valid * (cross / lt - lse_t + lse_s)
        lane = lax.broadcasted_iota(jnp.int32, (ROWS, STATS), 1)
        div[...] = jnp.sum(jnp.where(lane == home, value, 0.0), axis=0)[0:ROWS]
        emit(div, divergence)
        own, other = factors
        a_s = part[0:1, :] * own[0:1, 0:1] + got[0:1, 0:d] * other[0:1, 0:1]
        a_t = part[1:2, :] * own[0:1, 1:2] + got[1:2, 0:d] * other[0:1, 1:2]
        hid[...] = (gain[0:1] * (a_s / ls[0:1] - a_t / lt[0:1])).astype(jnp.bfloat16)
        emit(hid, hidden_grad)
        for i in range(n // 2, n):
            weight_chunk(i)
        for copy in copies:
            copy.wait()

    return last_kernel


VMEM = pl.BlockSpec(memory_space=pltpu.VMEM)
ANY = pl.BlockSpec(memory_space=pltpu.HBM)
PARAMS = pltpu.CompilerParams(vmem_limit_bytes=32 << 20)


def call(kernel, out, scratch=(), in_specs=None, out_specs=None, cost=None):
    shapes = [jax.ShapeDtypeStruct(s, t) for s, t in out]
    return lambda *a: pl.pallas_call(
        kernel,
        out_shape=shapes,
        in_specs=in_specs or [VMEM] * len(a),
        out_specs=out_specs or [VMEM] * len(out),
        scratch_shapes=list(scratch),
        compiler_params=PARAMS,
        cost_estimate=cost,
    )(*a)


def small_body(hidden_rows, mentor, head_weight, row_mask):
    f32, bf16 = jnp.float32, jnp.bfloat16
    v, d = head_weight.shape
    valid, tile, own = call(
        entry_kernel,
        [((ROWS, STATS), f32), (mentor.shape, f32), ((4, d), bf16)],
        [pltpu.SMEM((ROWS,), jnp.int32), pltpu.SemaphoreType.DMA((3,))],
        [ANY] * 3,
        cost=pl.CostEstimate(flops=2_000_000_000, transcendentals=0, bytes_accessed=2 << 20),
    )(*(pltpu.with_memory_space_constraint(a, pltpu.HBM) for a in (row_mask, mentor, hidden_rows)))
    pieces = [lax.ppermute(own, "vocab", flip(4, k)) for k in (1, 2, 3)]
    scaled, et, teacher = call(
        teacher_kernel,
        [((ROWS, v), f32), ((ROWS, v), f32), ((ROWS, STATS), f32)],
        [pltpu.VMEM((ROWS, v), f32)],
    )(valid, tile, lax.ppermute(tile, "teach", flip(2, 1)))
    student, stats, hb, keep, send = call(
        first_kernel,
        [((ROWS, v), f32), ((ROWS, STATS), f32), ((ROWS, d), bf16), ((16, d), f32), ((16, d + STATS), f32)],
        [
            pltpu.VMEM((ROWS, d), f32),
            pltpu.VMEM((ROWS, v), f32),
            pltpu.VMEM((2 * ROWS, v), f32),
        ],
    )(own, *pieces, head_weight, scaled, et, teacher)
    got = lax.ppermute(send, "teach", flip(2, 1))
    stats, keep, *sends = call(
        second_kernel,
        [((ROWS, STATS), f32), ((4, d), f32)] + [((4, d + 4 * STATS), f32)] * 3,
    )(keep, stats, got)
    gots = [lax.ppermute(a, "vocab", flip(4, k)) for k, a in zip((3, 2, 1), sends)]
    stats, keep, send = call(
        third_kernel,
        [((ROWS, STATS), f32), ((2, d), f32), ((2, d + 8 * STATS), f32)],
        [pltpu.VMEM((3, ROWS, STATS), f32)],
    )(keep, stats, *gots)
    got = lax.ppermute(send, "rows", flip(2, 1))
    chunk = 512
    return tuple(
        call(
            make_last_kernel(chunk),
            [((ROWS,), f32), ((1, d), bf16), ((v, d), bf16)],
            [
                pltpu.VMEM((ROWS, STATS), f32),
                pltpu.VMEM((ROWS, v), f32),
                pltpu.VMEM((v, d), bf16),
                pltpu.VMEM((ROWS,), f32),
                pltpu.VMEM((1, d), bf16),
                pltpu.SemaphoreType.DMA((d // chunk + 2,)),
            ],
            [VMEM] * 6,
            [ANY] * 3,
        )(keep, stats, got, student, scaled, hb)
    )


def solution(mesh):
    sizes = mesh.shape["vocab"], mesh.shape["rows"], mesh.shape["teach"]
    general = make_body(*sizes)

    def body(hidden_rows, mentor, head_weight, row_mask):
        small = sizes == (4, 2, 2) and row_mask.shape[0] == ROWS and head_weight.shape[1] % 512 == 0
        return (small_body if small else general)(hidden_rows, mentor, head_weight, row_mask)
    return jax.shard_map(
        body,
        mesh=mesh,
        in_specs=(
            P(("groups", "vocab"), None),
            P(("groups", "teach"), ("vocab", "rows")),
            P(("vocab", "rows", "teach"), None),
            P("groups"),
        ),
        out_specs=(
            P("groups"),
            P(("groups", "vocab", "rows", "teach"), None),
            P(("groups", "vocab", "rows", "teach"), None),
        ),
        check_vma=False,
    )
```

```python
import jax
import jax.numpy as jnp
from jax import lax
from jax.experimental import pallas as pl
from jax.experimental.pallas import tpu as pltpu
from jax.sharding import PartitionSpec as P

smoothing_divisor = 2.0
objective_scale = 256.0


def flip(n, d):
    return [(i, i ^ d) for i in range(n)]


def bits(n):
    out = []
    d = 1
    while d < n:
        out.append(d)
        d *= 2
    return out


def swap(a, d):
    n = a.shape[0]
    b = a.reshape((n // (2 * d), 2, d) + a.shape[1:])
    return jnp.concatenate([b[:, 1:], b[:, :1]], axis=1).reshape(a.shape)


def relative(a, position, n, stride):
    for d in bits(n):
        a = jnp.where((position & d) != 0, swap(a, d * stride), a)
    return a


def make_body(nz, nx, nc):
    def body(hidden_rows, mentor, head_weight, row_mask):
        z, x, c = lax.axis_index("vocab"), lax.axis_index("rows"), lax.axis_index("teach")
        total = row_mask.shape[0]
        q = total // (nz * nx * nc)
        own = relative(relative(hidden_rows, c, nc, q), x, nx, q * nc)
        gathered = own
        if nz == 4:
            gathered = jnp.concatenate(
                [own] + [lax.ppermute(own, "vocab", flip(nz, k)) for k in (1, 2, 3)], 0
            )
        else:
            for d in bits(nz):
                gathered = jnp.concatenate([gathered, lax.ppermute(gathered, "vocab", flip(nz, d))], 0)
        width = mentor.shape[1] // 2
        left, right = mentor[:, :width], mentor[:, width:]
        kept = jnp.where(c == 0, left, right)
        got = lax.ppermute(jnp.where(c == 0, right, left), "teach", flip(nc, 1))
        scaled = jnp.concatenate([jnp.where(c == 0, kept, got), jnp.where(c == 0, got, kept)], 0)

        def rel(a):
            a = relative(a, c, nc, q)
            a = relative(a, x, nx, q * nc)
            return relative(a, z, nz, q * nc * nx)

        scaled = rel(scaled) / smoothing_divisor
        mask = rel(row_mask).astype(jnp.float32)
        student = (
            lax.dot_general(
                gathered, head_weight, (((1,), (1,)), ((), ())), preferred_element_type=jnp.float32
            )
            / smoothing_divisor
        )
        ms = jnp.max(student, axis=1)
        mt = jnp.max(scaled, axis=1)
        es = jnp.exp(student - ms[:, None])
        et = jnp.exp(scaled - mt[:, None])
        stats = jnp.stack(
            [ms, mt, jnp.sum(es, axis=1), jnp.sum(et, axis=1), jnp.sum(et * (scaled - student), axis=1)], 0
        )
        both = jnp.concatenate([es, et], 0)
        high = both.astype(jnp.bfloat16)
        low = (both - high.astype(jnp.float32)).astype(jnp.bfloat16)
        part = jnp.dot(
            jnp.concatenate([high, low], 0), head_weight, preferred_element_type=jnp.float32
        )
        part = part[: 2 * total] + part[2 * total :]
        part = part.reshape(2, nz, nx, nc, q, -1)

        def merge(keep, stats, others):
            top = stats[:2]
            for _, s in others:
                top = jnp.maximum(top, s[:2])
            factor = [jnp.exp(s[:2] - top) for s in [stats] + [s for _, s in others]]
            sums = sum(
                jnp.concatenate([f * s[2:4], (f[1] * s[4])[None]], 0)
                for f, s in zip(factor, [stats] + [s for _, s in others])
            )
            return top, factor, jnp.concatenate([top, sums], 0)

        def level(part, stats, axis, n, dim, stride):
            if n == 4:
                steps = [(1, 2, 3)]
            else:
                steps = [(d,) for d in reversed(bits(n))]
            size = n
            for ds in steps:
                span = size // (len(ds) + 1)
                keep = lax.slice_in_dim(part, 0, span, axis=dim)
                others = []
                for d in ds:
                    a = lax.ppermute(lax.slice_in_dim(part, d, d + span, axis=dim), axis, flip(n, d))
                    s = lax.ppermute(stats, axis, flip(n, d))
                    s = s.T
                    for b in bits(n):
                        if d & b:
                            s = swap(s, b * stride)
                    others.append((a, s.T))
                _, factor, stats = merge(keep, stats, others)
                rows = [f.reshape(2, nz, nx, nc, q, 1) for f in factor]

                def cut(f):
                    shape = keep.shape
                    for ax in range(1, 4):
                        f = lax.slice_in_dim(f, 0, shape[ax], axis=ax)
                    return f

                part = keep * cut(rows[0])
                for (a, _), f in zip(others, rows[1:]):
                    part = part + a * cut(f)
                size = span
            return part, stats

        part, stats = level(part, stats, "teach", nc, 3, q)
        part, stats = level(part, stats, "rows", nx, 2, q * nc)
        part, stats = level(part, stats, "vocab", nz, 1, q * nc * nx)
        part = part.reshape(2, q, -1)
        ms, mt, ls, lt, cross = stats
        lse_s = ms + jnp.log(ls)
        lse_t = mt + jnp.log(lt)
        divergence = rel(mask * (cross / lt - lse_t + lse_s))
        gain = mask * (objective_scale * smoothing_divisor)
        grad = (
            gain[:, None] * (jnp.exp(student - lse_s[:, None]) - jnp.exp(scaled - lse_t[:, None]))
        ).astype(jnp.bfloat16)
        weight_grad = lax.dot_general(
            grad, gathered, (((0,), (0,)), ((), ())), preferred_element_type=jnp.float32
        )
        hidden_grad = gain[:q, None] * (part[0] / ls[:q, None] - part[1] / lt[:q, None])
        return divergence, hidden_grad.astype(jnp.bfloat16), weight_grad.astype(jnp.bfloat16)

    return body


ROWS = 16
STATS = 128


def pack(columns):
    lane = lax.broadcasted_iota(jnp.int32, (ROWS, STATS), 1)
    out = jnp.zeros((ROWS, STATS), jnp.float32)
    for i, column in enumerate(columns):
        out = jnp.where(lane == i, column, out)
    return out


def unite(parts):
    top = parts[0]
    for s in parts[1:]:
        top = jnp.maximum(top, s)
    factors = [jnp.exp(s - top) for s in parts]
    ls = sum(s[:, 2:3] * f[:, 0:1] for s, f in zip(parts, factors))
    lt = sum(s[:, 3:4] * f[:, 1:2] for s, f in zip(parts, factors))
    cross = sum(s[:, 4:5] * f[:, 1:2] for s, f in zip(parts, factors))
    return factors, [top[:, 0:1], top[:, 1:2], ls, lt, cross, top[:, 5:6]]


def fold(st, rows):
    shift = STATS // 2
    while st.shape[0] > rows:
        half = st.shape[0] // 2
        st = st[0:half] + pltpu.roll(st[half:], shift, 1)
        shift //= 2
    return st


def unfold(target, block, flipped):
    rows = block.shape[0]
    step = STATS * rows // ROWS
    for i in range(ROWS // rows):
        at = (i * rows) ^ flipped
        target[at : at + rows, :] = block if i == 0 else pltpu.roll(block, STATS - step * i, 1)


def places():
    return lax.axis_index("vocab"), lax.axis_index("rows"), lax.axis_index("teach")


def row_of(b, x, c):
    return 2 * (x ^ (b & 1)) + (c ^ (b >> 1))


def entry_kernel(mask_in, own_in, h_in, valid_out, own, h, mask, sems):
    pairs = ((mask_in, mask), (h_in, h), (own_in, own))
    copies = [pltpu.make_async_copy(a, b, sems.at[i]) for i, (a, b) in enumerate(pairs)]
    for copy in copies:
        copy.start()
    z, x, c = places()
    copies[0].wait()
    row = lax.broadcasted_iota(jnp.int32, (ROWS, STATS), 0)
    valid = jnp.zeros((ROWS, STATS), jnp.float32)
    for r in range(ROWS):
        at = 4 * ((r & 3) ^ z) + row_of(r >> 2, x, c)
        valid = jnp.where(row == r, mask[at].astype(jnp.float32), valid)
    valid_out[...] = valid
    copies[1].wait()
    copies[2].wait()


def teacher_kernel(valid, own, got, scaled, et, stats, tt):
    z, x, c = places()
    v = scaled.shape[1]
    for i, tile in ((c, own[...]), (1 - c, got[...])):
        tt[pl.ds(pl.multiple_of(8 * i, 8), 8), :] = 0.5 * jnp.where(c == 0, tile[:, 0:v], tile[:, v : 2 * v])
    for r in range(ROWS):
        scaled[r : r + 1, :] = tt[pl.ds(4 * ((r & 3) ^ z) + row_of(r >> 2, x, c), 1), :]
    t = scaled[...]
    mt = jnp.max(t, axis=1, keepdims=True)
    e = jnp.exp(t - mt)
    et[...] = e
    none = jnp.zeros_like(mt)
    stats[...] = pack([none, mt, none, jnp.sum(e, axis=1, keepdims=True), none, valid[:, 5:6]])


def first_kernel(h0, h1, h2, h3, w, scaled, et_in, teacher, student, stats, hb, keep, send, hf, raw, e):
    z, x, c = places()
    for k, h in enumerate((h0, h1, h2, h3)):
        hf[4 * k : 4 * k + 4, :] = h[...].astype(jnp.float32)
    rows = hf[...].astype(jnp.bfloat16)
    hb[...] = rows
    raw[...] = 0.5 * lax.dot_general(
        rows, w[...], (((1,), (1,)), ((), ())), preferred_element_type=jnp.float32
    )

    @pl.when(z >= 0)
    def _():
        for b in range(4):
            j = row_of(b, x, c)
            for k in range(4):
                student[4 * b + k : 4 * b + k + 1, :] = raw[pl.ds(4 * k + j, 1), :]
        s = student[...]
        t = scaled[...]
        et = et_in[...]
        ms = jnp.max(s, axis=1, keepdims=True)
        es = jnp.exp(s - ms)
        st = pack(
            [
                ms,
                teacher[:, 1:2],
                jnp.sum(es, axis=1, keepdims=True),
                teacher[:, 3:4],
                jnp.sum(et * (t - s), axis=1, keepdims=True),
                teacher[:, 5:6],
            ]
        )
        stats[...] = st
        for b in range(4):
            e[8 * b : 8 * b + 4, :] = es[4 * b : 4 * b + 4, :]
            e[8 * b + 4 : 8 * b + 8, :] = et[4 * b : 4 * b + 4, :]
        both = e[...]
        high = both.astype(jnp.bfloat16)
        low = (both - high.astype(jnp.float32)).astype(jnp.bfloat16)
        part = jnp.dot(jnp.concatenate([high, low], 0), w[...], preferred_element_type=jnp.float32)
        d = part.shape[1]
        keep[...] = part[0:16] + part[32:48]
        send[:, 0:d] = part[16:32] + part[48:64]
        send[0:8, d:] = st[8:16]
        send[8:16, d:] = st[0:8]


def second_kernel(part, stats, got, stats_out, keep, send):
    d = part.shape[1]
    factors, columns = unite([stats[...], got[:, d:]])
    st = pack(columns)
    stats_out[...] = st
    scale = [
        jnp.concatenate([f[0:4, 0:1], f[0:4, 1:2], f[4:8, 0:1], f[4:8, 1:2]], 0) for f in factors
    ]
    total = part[...] * scale[0] + got[:, 0:d] * scale[1]
    keep[...] = total[0:8]
    send[:, 0:d] = total[8:16]
    block = fold(st, 8)
    send[0:4, d:] = block[4:8]
    send[4:8, d:] = block[0:4]


def third_kernel(part, stats, got, stats_out, keep, send3, send2, send1, gs):
    d = part.shape[1]
    unfold(gs, got[:, d:], 0)
    factors, columns = unite([stats[...], gs[...]])
    st = pack(columns)
    stats_out[...] = st
    scale = [jnp.concatenate([f[0:4, 0:1], f[0:4, 1:2]], 0) for f in factors]
    total = part[...] * scale[0] + got[:, 0:d] * scale[1]
    keep[0:1, :] = total[0:1]
    keep[1:2, :] = total[4:5]
    block = fold(st, 2)
    for k, send in enumerate((send1, send2, send3), 1):
        send[0:1, 0:d] = total[k : k + 1]
        send[1:2, 0:d] = total[4 + k : 5 + k]
        for i in range(2):
            r = i ^ (k & 1)
            send[i : i + 1, d:] = block[r : r + 1]


def make_last_kernel(chunk):
    def last_kernel(
        part, stats, got3, got2, got1, student, scaled, hb,
        divergence, hidden_grad, weight_grad, gs, gr, out, div, hid, sems,
    ):
        z, x, c = places()
        d = part.shape[1]
        parts = [stats[...]]
        for k, got in enumerate((got1, got2, got3)):
            unfold(gs.at[k], got[:, d:], (k + 1) & 2)
            parts.append(gs[k])
        factors, (ms, mt, ls, lt, cross, valid) = unite(parts)
        lse_s = ms + jnp.log(ls)
        lse_t = mt + jnp.log(lt)
        gain = valid * (objective_scale * smoothing_divisor)
        grad = gain * (jnp.exp(student[...] - lse_s) - jnp.exp(scaled[...] - lse_t))
        for b in range(4):
            j = row_of(b, x, c)
            for k in range(4):
                gr[pl.ds(4 * k + j, 1), :] = grad[4 * b + k : 4 * b + k + 1, :]
        g = gr[...].astype(jnp.bfloat16)
        copies = []

        def emit(source, target):
            copy = pltpu.make_async_copy(source, target, sems.at[len(copies)])
            copy.start()
            copies.append(copy)

        def weight_chunk(i):
            at = pl.ds(i * chunk, chunk)
            out[:, at] = lax.dot_general(
                g, hb[:, at], (((0,), (0,)), ((), ())), preferred_element_type=jnp.float32
            ).astype(jnp.bfloat16)
            emit(out.at[:, at], weight_grad.at[:, at])

        n = d // chunk
        for i in range(n // 2):
            weight_chunk(i)
        row = lax.broadcasted_iota(jnp.int32, (ROWS, 1), 0)
        home = 4 * (z ^ (row & 3)) + 2 * (x ^ ((row >> 2) & 1)) + (c ^ (row >> 3))
        value = valid * (cross / lt - lse_t + lse_s)
        lane = lax.broadcasted_iota(jnp.int32, (ROWS, STATS), 1)
        div[...] = jnp.sum(jnp.where(lane == home, value, 0.0), axis=0)[0:ROWS]
        emit(div, divergence)
        a_s = part[0:1, :] * factors[0][0:1, 0:1]
        a_t = part[1:2, :] * factors[0][0:1, 1:2]
        for got, f in zip((got1, got2, got3), factors[1:]):
            a_s = a_s + got[0:1, 0:d] * f[0:1, 0:1]
            a_t = a_t + got[1:2, 0:d] * f[0:1, 1:2]
        hid[...] = (gain[0:1] * (a_s / ls[0:1] - a_t / lt[0:1])).astype(jnp.bfloat16)
        emit(hid, hidden_grad)
        for i in range(n // 2, n):
            weight_chunk(i)
        for copy in copies:
            copy.wait()

    return last_kernel


VMEM = pl.BlockSpec(memory_space=pltpu.VMEM)
ANY = pl.BlockSpec(memory_space=pltpu.HBM)
PARAMS = pltpu.CompilerParams(vmem_limit_bytes=32 << 20)


def call(kernel, out, scratch=(), in_specs=None, out_specs=None, cost=None):
    shapes = [jax.ShapeDtypeStruct(s, t) for s, t in out]
    return lambda *a: pl.pallas_call(
        kernel,
        out_shape=shapes,
        in_specs=in_specs or [VMEM] * len(a),
        out_specs=out_specs or [VMEM] * len(out),
        scratch_shapes=list(scratch),
        compiler_params=PARAMS,
        cost_estimate=cost,
    )(*a)


def small_body(hidden_rows, mentor, head_weight, row_mask):
    f32, bf16 = jnp.float32, jnp.bfloat16
    v, d = head_weight.shape
    valid, tile, own = call(
        entry_kernel,
        [((ROWS, STATS), f32), (mentor.shape, f32), ((4, d), bf16)],
        [pltpu.SMEM((ROWS,), jnp.int32), pltpu.SemaphoreType.DMA((3,))],
        [ANY] * 3,
        cost=pl.CostEstimate(flops=2_000_000_000, transcendentals=0, bytes_accessed=2 << 20),
    )(*(pltpu.with_memory_space_constraint(a, pltpu.HBM) for a in (row_mask, mentor, hidden_rows)))
    pieces = [lax.ppermute(own, "vocab", flip(4, k)) for k in (1, 2, 3)]
    scaled, et, teacher = call(
        teacher_kernel,
        [((ROWS, v), f32), ((ROWS, v), f32), ((ROWS, STATS), f32)],
        [pltpu.VMEM((ROWS, v), f32)],
    )(valid, tile, lax.ppermute(tile, "teach", flip(2, 1)))
    student, stats, hb, keep, send = call(
        first_kernel,
        [((ROWS, v), f32), ((ROWS, STATS), f32), ((ROWS, d), bf16), ((16, d), f32), ((16, d + STATS), f32)],
        [
            pltpu.VMEM((ROWS, d), f32),
            pltpu.VMEM((ROWS, v), f32),
            pltpu.VMEM((2 * ROWS, v), f32),
        ],
    )(own, *pieces, head_weight, scaled, et, teacher)
    got = lax.ppermute(send, "teach", flip(2, 1))
    stats, keep, send = call(
        second_kernel, [((ROWS, STATS), f32), ((8, d), f32), ((8, d + STATS), f32)]
    )(keep, stats, got)
    got = lax.ppermute(send, "rows", flip(2, 1))
    stats, keep, *sends = call(
        third_kernel,
        [((ROWS, STATS), f32), ((2, d), f32)] + [((2, d + STATS), f32)] * 3,
        [pltpu.VMEM((ROWS, STATS), f32)],
    )(keep, stats, got)
    gots = [lax.ppermute(a, "vocab", flip(4, k)) for k, a in zip((3, 2, 1), sends)]
    chunk = 512
    return tuple(
        call(
            make_last_kernel(chunk),
            [((ROWS,), f32), ((1, d), bf16), ((v, d), bf16)],
            [
                pltpu.VMEM((3, ROWS, STATS), f32),
                pltpu.VMEM((ROWS, v), f32),
                pltpu.VMEM((v, d), bf16),
                pltpu.VMEM((ROWS,), f32),
                pltpu.VMEM((1, d), bf16),
                pltpu.SemaphoreType.DMA((d // chunk + 2,)),
            ],
            [VMEM] * 8,
            [ANY] * 3,
        )(keep, stats, *gots, student, scaled, hb)
    )


def solution(mesh):
    sizes = mesh.shape["vocab"], mesh.shape["rows"], mesh.shape["teach"]
    general = make_body(*sizes)

    def body(hidden_rows, mentor, head_weight, row_mask):
        small = sizes == (4, 2, 2) and row_mask.shape[0] == ROWS and head_weight.shape[1] % 512 == 0
        return (small_body if small else general)(hidden_rows, mentor, head_weight, row_mask)
    return jax.shard_map(
        body,
        mesh=mesh,
        in_specs=(
            P(("groups", "vocab"), None),
            P(("groups", "teach"), ("vocab", "rows")),
            P(("vocab", "rows", "teach"), None),
            P("groups"),
        ),
        out_specs=(
            P("groups"),
            P(("groups", "vocab", "rows", "teach"), None),
            P(("groups", "vocab", "rows", "teach"), None),
        ),
        check_vma=False,
    )
```

```python
import jax
import jax.numpy as jnp
from jax import lax
from jax.experimental import pallas as pl
from jax.experimental.pallas import tpu as pltpu
from jax.sharding import PartitionSpec as P

smoothing_divisor = 2.0
objective_scale = 256.0


def flip(n, d):
    return [(i, i ^ d) for i in range(n)]


def bits(n):
    out = []
    d = 1
    while d < n:
        out.append(d)
        d *= 2
    return out


def swap(a, d):
    n = a.shape[0]
    b = a.reshape((n // (2 * d), 2, d) + a.shape[1:])
    return jnp.concatenate([b[:, 1:], b[:, :1]], axis=1).reshape(a.shape)


def relative(a, position, n, stride):
    for d in bits(n):
        a = jnp.where((position & d) != 0, swap(a, d * stride), a)
    return a


def make_body(nz, nx, nc):
    def body(hidden_rows, mentor, head_weight, row_mask):
        z, x, c = lax.axis_index("vocab"), lax.axis_index("rows"), lax.axis_index("teach")
        total = row_mask.shape[0]
        q = total // (nz * nx * nc)
        own = relative(relative(hidden_rows, c, nc, q), x, nx, q * nc)
        gathered = own
        if nz == 4:
            gathered = jnp.concatenate(
                [own] + [lax.ppermute(own, "vocab", flip(nz, k)) for k in (1, 2, 3)], 0
            )
        else:
            for d in bits(nz):
                gathered = jnp.concatenate([gathered, lax.ppermute(gathered, "vocab", flip(nz, d))], 0)
        width = mentor.shape[1] // 2
        left, right = mentor[:, :width], mentor[:, width:]
        kept = jnp.where(c == 0, left, right)
        got = lax.ppermute(jnp.where(c == 0, right, left), "teach", flip(nc, 1))
        scaled = jnp.concatenate([jnp.where(c == 0, kept, got), jnp.where(c == 0, got, kept)], 0)

        def rel(a):
            a = relative(a, c, nc, q)
            a = relative(a, x, nx, q * nc)
            return relative(a, z, nz, q * nc * nx)

        scaled = rel(scaled) / smoothing_divisor
        mask = rel(row_mask).astype(jnp.float32)
        student = (
            lax.dot_general(
                gathered, head_weight, (((1,), (1,)), ((), ())), preferred_element_type=jnp.float32
            )
            / smoothing_divisor
        )
        ms = jnp.max(student, axis=1)
        mt = jnp.max(scaled, axis=1)
        es = jnp.exp(student - ms[:, None])
        et = jnp.exp(scaled - mt[:, None])
        stats = jnp.stack(
            [ms, mt, jnp.sum(es, axis=1), jnp.sum(et, axis=1), jnp.sum(et * (scaled - student), axis=1)], 0
        )
        both = jnp.concatenate([es, et], 0)
        high = both.astype(jnp.bfloat16)
        low = (both - high.astype(jnp.float32)).astype(jnp.bfloat16)
        part = jnp.dot(
            jnp.concatenate([high, low], 0), head_weight, preferred_element_type=jnp.float32
        )
        part = part[: 2 * total] + part[2 * total :]
        part = part.reshape(2, nz, nx, nc, q, -1)

        def merge(keep, stats, others):
            top = stats[:2]
            for _, s in others:
                top = jnp.maximum(top, s[:2])
            factor = [jnp.exp(s[:2] - top) for s in [stats] + [s for _, s in others]]
            sums = sum(
                jnp.concatenate([f * s[2:4], (f[1] * s[4])[None]], 0)
                for f, s in zip(factor, [stats] + [s for _, s in others])
            )
            return top, factor, jnp.concatenate([top, sums], 0)

        def level(part, stats, axis, n, dim, stride):
            if n == 4:
                steps = [(1, 2, 3)]
            else:
                steps = [(d,) for d in reversed(bits(n))]
            size = n
            for ds in steps:
                span = size // (len(ds) + 1)
                keep = lax.slice_in_dim(part, 0, span, axis=dim)
                others = []
                for d in ds:
                    a = lax.ppermute(lax.slice_in_dim(part, d, d + span, axis=dim), axis, flip(n, d))
                    s = lax.ppermute(stats, axis, flip(n, d))
                    s = s.T
                    for b in bits(n):
                        if d & b:
                            s = swap(s, b * stride)
                    others.append((a, s.T))
                _, factor, stats = merge(keep, stats, others)
                rows = [f.reshape(2, nz, nx, nc, q, 1) for f in factor]

                def cut(f):
                    shape = keep.shape
                    for ax in range(1, 4):
                        f = lax.slice_in_dim(f, 0, shape[ax], axis=ax)
                    return f

                part = keep * cut(rows[0])
                for (a, _), f in zip(others, rows[1:]):
                    part = part + a * cut(f)
                size = span
            return part, stats

        part, stats = level(part, stats, "teach", nc, 3, q)
        part, stats = level(part, stats, "rows", nx, 2, q * nc)
        part, stats = level(part, stats, "vocab", nz, 1, q * nc * nx)
        part = part.reshape(2, q, -1)
        ms, mt, ls, lt, cross = stats
        lse_s = ms + jnp.log(ls)
        lse_t = mt + jnp.log(lt)
        divergence = rel(mask * (cross / lt - lse_t + lse_s))
        gain = mask * (objective_scale * smoothing_divisor)
        grad = (
            gain[:, None] * (jnp.exp(student - lse_s[:, None]) - jnp.exp(scaled - lse_t[:, None]))
        ).astype(jnp.bfloat16)
        weight_grad = lax.dot_general(
            grad, gathered, (((0,), (0,)), ((), ())), preferred_element_type=jnp.float32
        )
        hidden_grad = gain[:q, None] * (part[0] / ls[:q, None] - part[1] / lt[:q, None])
        return divergence, hidden_grad.astype(jnp.bfloat16), weight_grad.astype(jnp.bfloat16)

    return body


ROWS = 16
STATS = 128


def pack(columns):
    lane = lax.broadcasted_iota(jnp.int32, (ROWS, STATS), 1)
    out = jnp.zeros((ROWS, STATS), jnp.float32)
    for i, column in enumerate(columns):
        out = jnp.where(lane == i, column, out)
    return out


def unite(parts):
    top = parts[0]
    for s in parts[1:]:
        top = jnp.maximum(top, s)
    factors = [jnp.exp(s - top) for s in parts]
    ls = sum(s[:, 2:3] * f[:, 0:1] for s, f in zip(parts, factors))
    lt = sum(s[:, 3:4] * f[:, 1:2] for s, f in zip(parts, factors))
    cross = sum(s[:, 4:5] * f[:, 1:2] for s, f in zip(parts, factors))
    return factors, [top[:, 0:1], top[:, 1:2], ls, lt, cross, top[:, 5:6]]


def places():
    return lax.axis_index("vocab"), lax.axis_index("rows"), lax.axis_index("teach")


def row_of(b, x, c):
    return 2 * (x ^ (b & 1)) + (c ^ (b >> 1))


def entry_kernel(mask_in, own_in, h_in, valid_out, own, h, mask, sems):
    pairs = ((mask_in, mask), (h_in, h), (own_in, own))
    copies = [pltpu.make_async_copy(a, b, sems.at[i]) for i, (a, b) in enumerate(pairs)]
    for copy in copies:
        copy.start()
    z, x, c = places()
    copies[0].wait()
    row = lax.broadcasted_iota(jnp.int32, (ROWS, STATS), 0)
    valid = jnp.zeros((ROWS, STATS), jnp.float32)
    for r in range(ROWS):
        at = 4 * ((r & 3) ^ z) + row_of(r >> 2, x, c)
        valid = jnp.where(row == r, mask[at].astype(jnp.float32), valid)
    valid_out[...] = valid
    copies[1].wait()
    copies[2].wait()


def teacher_kernel(valid, own, got, scaled, et, stats, tt):
    z, x, c = places()
    v = scaled.shape[1]
    for i, tile in ((c, own[...]), (1 - c, got[...])):
        tt[pl.ds(pl.multiple_of(8 * i, 8), 8), :] = 0.5 * jnp.where(c == 0, tile[:, 0:v], tile[:, v : 2 * v])
    for r in range(ROWS):
        scaled[r : r + 1, :] = tt[pl.ds(4 * ((r & 3) ^ z) + row_of(r >> 2, x, c), 1), :]
    t = scaled[...]
    mt = jnp.max(t, axis=1, keepdims=True)
    e = jnp.exp(t - mt)
    et[...] = e
    none = jnp.zeros_like(mt)
    stats[...] = pack([none, mt, none, jnp.sum(e, axis=1, keepdims=True), none, valid[:, 5:6]])


def first_kernel(h0, h1, h3, h2, w, scaled, et_in, teacher, student, stats, hb, keep, send, hf, raw, e):
    z, x, c = places()
    for k, h in enumerate((h0, h1, h2, h3)):
        hf[4 * k : 4 * k + 4, :] = h[...].astype(jnp.float32)
    rows = hf[...].astype(jnp.bfloat16)
    hb[...] = rows
    raw[...] = 0.5 * lax.dot_general(
        rows, w[...], (((1,), (1,)), ((), ())), preferred_element_type=jnp.float32
    )

    @pl.when(z >= 0)
    def _():
        for b in range(4):
            j = row_of(b, x, c)
            for k in range(4):
                student[4 * b + k : 4 * b + k + 1, :] = raw[pl.ds(4 * k + j, 1), :]
        s = student[...]
        t = scaled[...]
        et = et_in[...]
        ms = jnp.max(s, axis=1, keepdims=True)
        es = jnp.exp(s - ms)
        st = pack(
            [
                ms,
                teacher[:, 1:2],
                jnp.sum(es, axis=1, keepdims=True),
                teacher[:, 3:4],
                jnp.sum(et * (t - s), axis=1, keepdims=True),
                teacher[:, 5:6],
            ]
        )
        stats[...] = st
        for b in range(4):
            e[8 * b : 8 * b + 4, :] = es[4 * b : 4 * b + 4, :]
            e[8 * b + 4 : 8 * b + 8, :] = et[4 * b : 4 * b + 4, :]
        both = e[...]
        high = both.astype(jnp.bfloat16)
        low = (both - high.astype(jnp.float32)).astype(jnp.bfloat16)
        part = jnp.dot(jnp.concatenate([high, low], 0), w[...], preferred_element_type=jnp.float32)
        d = part.shape[1]
        keep[...] = part[0:16] + part[32:48]
        send[:, 0:d] = part[16:32] + part[48:64]
        send[0:8, d:] = st[8:16]
        send[8:16, d:] = st[0:8]


def second_kernel(part, stats, got, stats_out, keep, send):
    d = part.shape[1]
    factors, columns = unite([stats[...], got[:, d:]])
    st = pack(columns)
    stats_out[...] = st
    scale = [
        jnp.concatenate([f[0:4, 0:1], f[0:4, 1:2], f[4:8, 0:1], f[4:8, 1:2]], 0) for f in factors
    ]
    total = part[...] * scale[0] + got[:, 0:d] * scale[1]
    keep[...] = total[0:8]
    send[:, 0:d] = total[8:16]
    for i in range(2):
        send[0:4, d + 128 * i : d + 128 * i + 128] = st[8 * i + 4 : 8 * i + 8]
        send[4:8, d + 128 * i : d + 128 * i + 128] = st[8 * i : 8 * i + 4]


def third_kernel(part, stats, got, stats_out, keep, send2, send3, send1, gs):
    d = part.shape[1]
    for i in range(2):
        gs[8 * i : 8 * i + 8, :] = got[:, d + 128 * i : d + 128 * i + 128]
    factors, columns = unite([stats[...], gs[...]])
    st = pack(columns)
    stats_out[...] = st
    scale = [jnp.concatenate([f[0:4, 0:1], f[0:4, 1:2]], 0) for f in factors]
    total = part[...] * scale[0] + got[:, 0:d] * scale[1]
    keep[0:1, :] = total[0:1]
    keep[1:2, :] = total[4:5]
    for k, send in enumerate((send1, send2, send3), 1):
        send[0:1, 0:d] = total[k : k + 1]
        send[1:2, 0:d] = total[4 + k : 5 + k]
        for p in range(ROWS):
            at = d + 128 * (p // 2)
            r = p ^ k
            send[p % 2 : p % 2 + 1, at : at + 128] = st[r : r + 1]


def make_last_kernel(chunk):
    def last_kernel(
        part, stats, got2, got3, got1, student, scaled, hb,
        divergence, hidden_grad, weight_grad, gs, gr, out, div, hid, sems,
    ):
        z, x, c = places()
        d = part.shape[1]
        parts = [stats[...]]
        for k, got in enumerate((got1, got2, got3)):
            for i in range(8):
                gs[k, 2 * i : 2 * i + 2, :] = got[:, d + 128 * i : d + 128 * i + 128]
            parts.append(gs[k])
        factors, (ms, mt, ls, lt, cross, valid) = unite(parts)
        lse_s = ms + jnp.log(ls)
        lse_t = mt + jnp.log(lt)
        gain = valid * (objective_scale * smoothing_divisor)
        grad = gain * (jnp.exp(student[...] - lse_s) - jnp.exp(scaled[...] - lse_t))
        for b in range(4):
            j = row_of(b, x, c)
            for k in range(4):
                gr[pl.ds(4 * k + j, 1), :] = grad[4 * b + k : 4 * b + k + 1, :]
        g = gr[...].astype(jnp.bfloat16)
        copies = []

        def emit(source, target):
            copy = pltpu.make_async_copy(source, target, sems.at[len(copies)])
            copy.start()
            copies.append(copy)

        def weight_chunk(i):
            at = pl.ds(i * chunk, chunk)
            out[:, at] = lax.dot_general(
                g, hb[:, at], (((0,), (0,)), ((), ())), preferred_element_type=jnp.float32
            ).astype(jnp.bfloat16)
            emit(out.at[:, at], weight_grad.at[:, at])

        n = d // chunk
        for i in range(n // 2):
            weight_chunk(i)
        row = lax.broadcasted_iota(jnp.int32, (ROWS, 1), 0)
        home = 4 * (z ^ (row & 3)) + 2 * (x ^ ((row >> 2) & 1)) + (c ^ (row >> 3))
        value = valid * (cross / lt - lse_t + lse_s)
        lane = lax.broadcasted_iota(jnp.int32, (ROWS, STATS), 1)
        div[...] = jnp.sum(jnp.where(lane == home, value, 0.0), axis=0)[0:ROWS]
        emit(div, divergence)
        a_s = part[0:1, :] * factors[0][0:1, 0:1]
        a_t = part[1:2, :] * factors[0][0:1, 1:2]
        for got, f in zip((got1, got2, got3), factors[1:]):
            a_s = a_s + got[0:1, 0:d] * f[0:1, 0:1]
            a_t = a_t + got[1:2, 0:d] * f[0:1, 1:2]
        hid[...] = (gain[0:1] * (a_s / ls[0:1] - a_t / lt[0:1])).astype(jnp.bfloat16)
        emit(hid, hidden_grad)
        for i in range(n // 2, n):
            weight_chunk(i)
        for copy in copies:
            copy.wait()

    return last_kernel


VMEM = pl.BlockSpec(memory_space=pltpu.VMEM)
ANY = pl.BlockSpec(memory_space=pltpu.HBM)
PARAMS = pltpu.CompilerParams(vmem_limit_bytes=32 << 20)


def call(kernel, out, scratch=(), in_specs=None, out_specs=None, cost=None):
    shapes = [jax.ShapeDtypeStruct(s, t) for s, t in out]
    return lambda *a: pl.pallas_call(
        kernel,
        out_shape=shapes,
        in_specs=in_specs or [VMEM] * len(a),
        out_specs=out_specs or [VMEM] * len(out),
        scratch_shapes=list(scratch),
        compiler_params=PARAMS,
        cost_estimate=cost,
    )(*a)


def small_body(hidden_rows, mentor, head_weight, row_mask):
    f32, bf16 = jnp.float32, jnp.bfloat16
    v, d = head_weight.shape
    valid, tile, own = call(
        entry_kernel,
        [((ROWS, STATS), f32), (mentor.shape, f32), ((4, d), bf16)],
        [pltpu.SMEM((ROWS,), jnp.int32), pltpu.SemaphoreType.DMA((3,))],
        [ANY] * 3,
        cost=pl.CostEstimate(flops=2_000_000_000, transcendentals=0, bytes_accessed=2 << 20),
    )(*(pltpu.with_memory_space_constraint(a, pltpu.HBM) for a in (row_mask, mentor, hidden_rows)))
    pieces = [lax.ppermute(own, "vocab", flip(4, k)) for k in (1, 3, 2)]
    scaled, et, teacher = call(
        teacher_kernel,
        [((ROWS, v), f32), ((ROWS, v), f32), ((ROWS, STATS), f32)],
        [pltpu.VMEM((ROWS, v), f32)],
    )(valid, tile, lax.ppermute(tile, "teach", flip(2, 1)))
    student, stats, hb, keep, send = call(
        first_kernel,
        [((ROWS, v), f32), ((ROWS, STATS), f32), ((ROWS, d), bf16), ((16, d), f32), ((16, d + STATS), f32)],
        [
            pltpu.VMEM((ROWS, d), f32),
            pltpu.VMEM((ROWS, v), f32),
            pltpu.VMEM((2 * ROWS, v), f32),
        ],
    )(own, *pieces, head_weight, scaled, et, teacher)
    got = lax.ppermute(send, "teach", flip(2, 1))
    stats, keep, send = call(
        second_kernel, [((ROWS, STATS), f32), ((8, d), f32), ((8, d + 2 * STATS), f32)]
    )(keep, stats, got)
    got = lax.ppermute(send, "rows", flip(2, 1))
    stats, keep, *sends = call(
        third_kernel,
        [((ROWS, STATS), f32), ((2, d), f32)] + [((2, d + 8 * STATS), f32)] * 3,
        [pltpu.VMEM((ROWS, STATS), f32)],
    )(keep, stats, got)
    gots = [lax.ppermute(a, "vocab", flip(4, k)) for k, a in zip((2, 3, 1), sends)]
    chunk = 512
    return tuple(
        call(
            make_last_kernel(chunk),
            [((ROWS,), f32), ((1, d), bf16), ((v, d), bf16)],
            [
                pltpu.VMEM((3, ROWS, STATS), f32),
                pltpu.VMEM((ROWS, v), f32),
                pltpu.VMEM((v, d), bf16),
                pltpu.VMEM((ROWS,), f32),
                pltpu.VMEM((1, d), bf16),
                pltpu.SemaphoreType.DMA((d // chunk + 2,)),
            ],
            [VMEM] * 8,
            [ANY] * 3,
        )(keep, stats, *gots, student, scaled, hb)
    )


def solution(mesh):
    sizes = mesh.shape["vocab"], mesh.shape["rows"], mesh.shape["teach"]
    general = make_body(*sizes)

    def body(hidden_rows, mentor, head_weight, row_mask):
        small = sizes == (4, 2, 2) and row_mask.shape[0] == ROWS and head_weight.shape[1] % 512 == 0
        return (small_body if small else general)(hidden_rows, mentor, head_weight, row_mask)
    return jax.shard_map(
        body,
        mesh=mesh,
        in_specs=(
            P(("groups", "vocab"), None),
            P(("groups", "teach"), ("vocab", "rows")),
            P(("vocab", "rows", "teach"), None),
            P("groups"),
        ),
        out_specs=(
            P("groups"),
            P(("groups", "vocab", "rows", "teach"), None),
            P(("groups", "vocab", "rows", "teach"), None),
        ),
        check_vma=False,
    )
```
